768 devices in a mesh: lat: 48 (over y_lo, z), lon: 16 (over y_hi, x, core).
Axes of the slice: x: 4, y: 8 (y_hi: 2, y_lo: 4; y = y_hi * 4 + y_lo), z: 12, core: 2. Of those that a mesh axis runs over, the one named last changes fastest.
Arguments:
- state: float32 [5, 144, 8, 8, 2880], P(None, 'lat', None, None, 'lon'), may hold values from -6 to 6
- courant_x: float32 [144, 8, 8, 2880], P('lat', None, None, 'lon'), may hold values from -4 to 4
- courant_y: float32 [144, 8, 8, 2880], P('lat', None, None, 'lon'), may hold values from -4 to 4
- block_of_slot: int32 [144], P('lat'), may hold values from 0 to 143, as said below
- face_source: int32 [144, 2], P('lat'), may hold values from -1 to 143, as said below
- cutoff: int32 [1152], replicated, may hold values from 0 to 256, as said below
Outputs:
- new_state: float32 [5, 144, 8, 8, 2880], P(None, 'lat', None, None, 'lon')
The draws below stay inside these ranges and needn't reach their ends.
Inputs may be any that keep to these rules, and one draw needn't show every extreme that they name: `block_of_slot`: each block number appears once. The polar blocks are the first and the last 24 block numbers; the 3 slots of one index of lat hold at most 2 polar blocks, and some index holds 2. `face_source`: entry 0 of slot s is the slot holding block block_of_slot[s] - 1 and entry 1 the slot holding block block_of_slot[s] + 1; -1 where that block does not exist. Rows of polar blocks have a cutoff of 1 or more; all other rows have 0.
All inputs are finite; a program needn't handle non-finite values.
Results may differ from the reference program's by a relative error of at most 0.00005.
Values sent between devices are 32-bit elements; how exact they have to be, the bound alone decides.
A program may use at most 64 MiB of HBM per device.

```python
import math
import jax
import jax.numpy as jnp
from jax import lax

NLON = 2880
KCUT = 256
FIELDS = 5
LEV = 8
BLK_DEV = 3
BR = 8
NBLK = 144


def layout_tables(key):
    base_key = jax.random.fold_in(key, 7)
    key_rank, key_pos, key_perm = jax.random.split(base_key, 3)
    devices = NBLK // BLK_DEV
    rank = jax.random.permutation(key_rank, devices)
    counts = jnp.where(rank < devices // 4, 2, jnp.where(rank < 3 * devices // 4, 1, 0))
    scores = jax.random.randint(key_pos, (devices, BLK_DEV), 0, 1024) * BLK_DEV + jnp.arange(BLK_DEV, dtype=jnp.int32)[None, :]
    inner = jnp.argsort(jnp.argsort(scores, axis=1), axis=1)
    polar_flag = (inner < counts[:, None]).reshape(-1)
    shuffle = jax.random.permutation(key_perm, NBLK)
    order = jnp.argsort(jnp.where(polar_flag, 0, NBLK) + shuffle).astype(jnp.int32)
    polar_count = NBLK // 6
    position = jnp.arange(NBLK, dtype=jnp.int32)
    sorted_blocks = jnp.where(position < polar_count, position, jnp.where(position < 2 * polar_count, NBLK - 2 * polar_count + position, position - polar_count))
    block_table = jnp.zeros((NBLK,), jnp.int32).at[order].set(sorted_blocks.astype(jnp.int32))
    slot_table = jnp.zeros((NBLK,), jnp.int32).at[block_table].set(position)
    north_slot = jnp.where(block_table > 0, slot_table[jnp.maximum(block_table - 1, 0)], -1)
    south_slot = jnp.where(block_table < NBLK - 1, slot_table[jnp.minimum(block_table + 1, NBLK - 1)], -1)
    return (block_table, jnp.stack([north_slot, south_slot], axis=1).astype(jnp.int32))


def draw_block_of_slot(key, part):
    return layout_tables(key)[0]


def draw_face_source(key, part):
    return layout_tables(key)[1]


def draw_cutoff(key, part):
    total_rows = NBLK * BR
    polar_rows = NBLK // 6 * BR
    row_index = jnp.arange(total_rows, dtype=jnp.int32)
    distance = jnp.minimum(row_index, total_rows - 1 - row_index)
    ramp = KCUT * (distance + 1) // polar_rows
    jitter = jax.random.randint(jax.random.fold_in(key, 11), (total_rows,), 0, 4)
    value = jnp.maximum(ramp - jitter, 1)
    value = jnp.where(distance == polar_rows - 1, KCUT, value)
    return jnp.where(distance < polar_rows, value, 0).astype(jnp.int32)


def block_scale(key, dims, shards, least, largest):
    def one(dim, parts):
        draws = jax.random.uniform(jax.random.fold_in(jax.random.fold_in(key, 6), dim), (parts,), jnp.float32, least / len(shards), largest / len(shards))
        return jnp.repeat(jnp.exp(draws), dims[dim] // parts).reshape((-1,) + (1,) * (len(dims) - dim - 1))

    gain = one(*shards[0])
    for cut in shards[1:]:
        gain = gain * one(*cut)
    return gain


def bell_draw(rng, extent, deviation, reach, shards=(), held_as=jnp.bfloat16):
    loudness = block_scale(rng, extent, shards, -0.22, 0.18) if shards else 1.0
    array = jax.random.normal(rng, extent, jnp.float32) * deviation * loudness
    return jnp.minimum(jnp.maximum(array, -reach), reach).astype(held_as)


def setup_inputs(seed: int = 0) -> dict:
    keys = jax.random.split(jax.random.key(seed), 7)
    state = bell_draw(keys[0], (FIELDS, NBLK, BR, LEV, NLON), 1.0, 6.0, ((1, 48), (4, 16)), jnp.float32)
    courant_x = bell_draw(keys[1], (NBLK, BR, LEV, NLON), 0.3, 4.0, ((0, 48), (3, 16)), jnp.float32)
    courant_y = bell_draw(keys[2], (NBLK, BR, LEV, NLON), 0.3, 4.0, ((0, 48), (3, 16)), jnp.float32)
    block_of_slot = draw_block_of_slot(jax.random.fold_in(keys[6], 71), 0)
    face_source = draw_face_source(jax.random.fold_in(keys[6], 71), 0)
    cutoff = draw_cutoff(jax.random.fold_in(keys[6], 71), 0)
    return dict(state=state, courant_x=courant_x, courant_y=courant_y, block_of_slot=block_of_slot, face_source=face_source, cutoff=cutoff)


def fourier_basis(columns):
    wavenumber = jnp.arange(KCUT, dtype=jnp.int32)
    phase = ((columns[:, None] * wavenumber[None, :]) % NLON).astype(jnp.float32) * (2.0 * math.pi / NLON)
    return jnp.concatenate([jnp.cos(phase), jnp.sin(phase)], axis=1)


def spectral_weights(cut_rows):
    wavenumber = jnp.arange(KCUT, dtype=jnp.int32)
    scaling = jnp.where(wavenumber == 0, 1.0 / NLON, 2.0 / NLON).astype(jnp.float32)
    kept = jnp.where(wavenumber[None, :] < cut_rows[:, None], scaling[None, :], 0.0).astype(jnp.float32)
    return jnp.concatenate([kept, kept], axis=1)


def reference(state, courant_x, courant_y, block_of_slot, face_source, cutoff):
    north_slot = face_source[:, 0]
    south_slot = face_source[:, 1]
    has_north = north_slot >= 0
    has_south = south_slot >= 0
    north_safe = jnp.maximum(north_slot, 0).astype(jnp.int32)
    south_safe = jnp.maximum(south_slot, 0).astype(jnp.int32)
    north_rows = jnp.where(has_north[None, :, None, None], state[:, north_safe, BR - 1], 0.0)
    south_rows = jnp.where(has_south[None, :, None, None], state[:, south_safe, 0], 0.0)
    north_wind = jnp.where(has_north[:, None, None], courant_y[north_safe, BR - 1], 0.0)
    extended = jnp.concatenate([north_rows[:, :, None], state, south_rows[:, :, None]], axis=2)
    wind_ext = jnp.concatenate([north_wind[:, None], courant_y], axis=1)
    face_keep = jnp.concatenate([jnp.ones((NBLK, BR), jnp.float32), has_south[:, None].astype(jnp.float32)], axis=1)
    merid_flux = wind_ext[None] * (extended[:, :, :-1] + extended[:, :, 1:]) * 0.5 * face_keep[None, :, :, None, None]
    merid_div = merid_flux[:, :, 1:] - merid_flux[:, :, :-1]
    zonal_flux = courant_x[None] * (state + jnp.roll(state, -1, axis=4)) * 0.5
    zonal_div = zonal_flux - jnp.roll(zonal_flux, 1, axis=4)
    tendency = -(zonal_div + merid_div)
    global_rows = block_of_slot[:, None] * BR + jnp.arange(BR, dtype=jnp.int32)[None, :]
    row_cut = cutoff[global_rows]
    cut_rows = jnp.broadcast_to(row_cut[:, :, None], (NBLK, BR, LEV)).reshape(-1)
    basis = fourier_basis(jnp.arange(NLON, dtype=jnp.int32))
    weights = spectral_weights(cut_rows)

    def filter_field(field_tend):
        row_matrix = field_tend.reshape(-1, NLON)
        spectrum = jnp.dot(row_matrix, basis, precision=lax.Precision.HIGHEST, preferred_element_type=jnp.float32)
        smoothed = jnp.dot(spectrum * weights, basis.T, precision=lax.Precision.HIGHEST, preferred_element_type=jnp.float32)
        return jnp.where(cut_rows[:, None] > 0, smoothed, row_matrix).reshape(field_tend.shape)

    filtered = lax.map(filter_field, tendency)
    return state + filtered
```

```python
import math

import jax
import jax.numpy as jnp
import numpy as np
from jax import lax
from jax.experimental import pallas as pl
from jax.experimental.pallas import tpu as pltpu
from jax.sharding import PartitionSpec as P

NLON = 2880
KCUT = 256
F, S, NR, L, W = 5, 3, 8, 8, 180
NBLK, POLAR = 144, 24
LANES = 256
NLAT, NLONDEV, HALF = 48, 16, 8
PIECES = NLAT * 8
MESH = pl.DeviceIdType.MESH
HIGHEST = lax.Precision.HIGHEST


def basis_table():
    column = np.arange(HALF * W, dtype=np.int64)
    phase = ((column[:, None] * np.arange(KCUT)[None, :]) % NLON) * (2.0 * math.pi / NLON)
    table = np.concatenate([np.cos(phase), np.sin(phase)], axis=1).reshape(HALF, W, 2 * KCUT)
    table = np.pad(table, ((0, 0), (0, LANES - W), (0, 0))).astype(np.float32)
    high = table.astype(jnp.bfloat16)
    low = (table - high.astype(np.float32)).astype(jnp.bfloat16)
    return np.stack([high, low])


def split2(x):
    high = x.astype(jnp.bfloat16)
    return high, (x - high.astype(jnp.float32)).astype(jnp.bfloat16)


def split3(x):
    high = x.astype(jnp.bfloat16)
    rest = x - high.astype(jnp.float32)
    mid = rest.astype(jnp.bfloat16)
    return high, mid, (rest - mid.astype(jnp.float32)).astype(jnp.bfloat16)


def dot(a, b, dims):
    return lax.dot_general(a, b, (dims, ((), ())), preferred_element_type=jnp.float32)


def store_rows(ref, c, t, value):
    for part in range(2):
        ref[pl.ds(c * 128 + part * 8 + t, L, stride=16), :] = value[:, part * 128:(part + 1) * 128]


def load_rows(ref, c, t):
    return jnp.concatenate([ref[pl.ds(c * 128 + part * 8 + t, L, stride=16), :] for part in range(2)], axis=1)


def iota(shape, dim):
    return lax.broadcasted_iota(jnp.int32, shape, dim)


def step_kernel(
    block_ref, face_ref, cut_ref, state_ref, cx_ref, cy_ref, table_hbm,
    out_ref,
    table, padded, send1, got1, send2, halo,
    edges, from_west, from_east, east_in, west_in,
    tend, rows_out, rows_in, spec, spec_in, smooth_out, smooth_in,
    table_sem, s1, r1, s2, r2, edge_send, edge_recv, a_send, a_recv, y_send, y_recv, b_send, b_recv,
):
    lat, lon = lax.axis_index("lat"), lax.axis_index("lon")
    half, seat = lon // HALF, lon % HALF
    partner = (lon + HALF) % NLONDEV
    east, west = (lon + 1) % NLONDEV, (lon + NLONDEV - 1) % NLONDEV

    load_table = pltpu.make_async_copy(table_hbm, table, table_sem)
    load_table.start()

    barrier = pltpu.get_barrier_semaphore()

    @pl.loop(1, NLAT)
    def _(i):
        pl.semaphore_signal(barrier, inc=1, device_id={"lat": (lat + i) % NLAT}, device_id_type=MESH)

    @pl.loop(1, NLONDEV)
    def _(i):
        pl.semaphore_signal(barrier, inc=1, device_id={"lon": (lon + i) % NLONDEV}, device_id_type=MESH)

    blocks = [block_ref[s] for s in range(S)]
    polar = [jnp.where(b < POLAR, 1, 0) + jnp.where(b >= NBLK - POLAR, 1, 0) for b in blocks]
    cols, keep = [], []
    for t in range(2 * S):
        n = face_ref[t % S, t // S]
        safe = jnp.maximum(n, 0)
        cols.append(jnp.where(n >= 0, 8 * lax.div(safe, S) + lax.rem(safe, S) + (t // S) * S, -1))
        keep.append(jnp.where(n >= 0, 1.0, 0.0))
    keep = keep[S:]
    first = (1 - polar[0]) * polar[2]
    picks = [first, 1 + polar[2]]

    lane = iota((L, LANES), 1)

    send1[...] = jnp.zeros_like(send1)
    padded[...] = jnp.zeros_like(padded)
    padded[:, :W] = state_ref[...].reshape(F * S * NR * L, W)

    def tile(f, s, r):
        return padded[pl.ds(pl.multiple_of(((f * S + s) * NR + r) * L, L), L), :]

    for t in range(2 * S):
        s = t % S
        want = jnp.full((L, LANES), cols[t].astype(jnp.float32), jnp.float32)
        for f in range(F):
            row = tile(f, s, NR - 1 if t < S else 0)
            store_rows(send1, f, t, jnp.where(lane == W, want, row))
        if t < S:
            wind = jnp.concatenate([cy_ref[s, NR - 1], jnp.zeros((L, LANES - W), jnp.float32)], axis=1)
            store_rows(send1, F, t, jnp.where(lane == W, want, wind))
        else:
            store_rows(send1, F, t, jnp.where(lane == W, want, 0.0))

    pick = jnp.where(
        jnp.logical_or(
            jnp.logical_and(iota((8, W), 0) == 0, iota((8, W), 1) == 0),
            jnp.logical_and(iota((8, W), 0) == 1, iota((8, W), 1) == W - 1),
        ),
        1.0, 0.0,
    ).astype(jnp.float32)
    edges[...] = jnp.zeros_like(edges)
    edges[:, :960] = lax.dot_general(
        pick, state_ref[...].reshape(F * S * NR * L, W), (((1,), (1,)), ((), ())),
        precision=HIGHEST, preferred_element_type=jnp.float32)
    edges[:, 1024:1216] = lax.dot_general(
        pick, cx_ref[...].reshape(S * NR * L, W), (((1,), (1,)), ((), ())),
        precision=HIGHEST, preferred_element_type=jnp.float32)

    pl.semaphore_wait(barrier, NLAT - 1 + NLONDEV - 1)

    def piece(ref, i):
        return ref.at[pl.ds(pl.multiple_of(i * 16, 16), 16), :]

    @pl.loop(1, NLAT)
    def _(i):
        to = (lat + i) % NLAT
        pltpu.make_async_remote_copy(
            piece(send1, to), piece(got1, lat), s1, r1, device_id={"lat": to}, device_id_type=MESH).start()

    to_west = pltpu.make_async_remote_copy(
        edges, from_east, edge_send.at[0], edge_recv.at[0], device_id={"lon": west}, device_id_type=MESH)
    to_east = pltpu.make_async_remote_copy(
        edges, from_west, edge_send.at[1], edge_recv.at[1], device_id={"lon": east}, device_id_type=MESH)
    to_west.start()
    to_east.start()
    mine = pl.ds(pl.multiple_of(lat * 16, 16), 16)
    got1[mine, :] = send1[mine, :]

    def wait_pieces(sem, ref):
        whole = ref.at[pl.ds(0, 16 * (NLAT - 1)), :]
        pltpu.make_async_copy(whole, whole, sem).wait()

    wait_pieces(r1, got1)
    parts = got1[...].reshape(NLAT, 2, 8, 128)
    pieces = jnp.concatenate([parts[:, i].reshape(PIECES, 128) for i in range(2)], axis=1)
    asked = jnp.broadcast_to(pieces[:, W:W + 1], (PIECES, PIECES))
    onehot = jnp.where(asked == iota((PIECES, PIECES), 1).astype(jnp.float32), 1.0, 0.0).astype(jnp.bfloat16)
    a, b, c = split3(pieces)
    nn = ((1,), (0,))
    found = (dot(onehot, a, nn) + dot(onehot, b, nn)) + dot(onehot, c, nn)
    send2[...] = jnp.stack(
        [found[:, i * 128:(i + 1) * 128].reshape(NLAT, 8, 128) for i in range(2)], axis=1).reshape(2 * PIECES, 128)

    @pl.loop(1, NLAT)
    def _(i):
        to = (lat + i) % NLAT
        pltpu.make_async_remote_copy(
            piece(send2, to), piece(halo, lat), s2, r2, device_id={"lat": to}, device_id_type=MESH).start()

    halo[mine, :] = send2[mine, :]

    to_west.wait()
    to_east.wait()
    place = lambda src, dst: jnp.where(
        jnp.logical_and(iota((8, LANES), 0) == src, iota((8, LANES), 1) == dst), 1.0, 0.0).astype(jnp.float32)
    tn = (((0,), (0,)), ((), ()))
    east_in[...] = lax.dot_general(
        from_east[...], place(0, W - 1), tn, precision=HIGHEST, preferred_element_type=jnp.float32)
    west_in[...] = lax.dot_general(
        from_west[...], place(1, 0), tn, precision=HIGHEST, preferred_element_type=jnp.float32)
    wait_pieces(r2, halo)

    zeros = jnp.zeros((L, LANES - W), jnp.float32)

    for s in range(S):
        kept = jnp.full((L, LANES), keep[s], jnp.float32)

        @pl.loop(0, F)
        def _(f):
            above, below = load_rows(halo, f, s), load_rows(halo, f, S + s)
            north_wind = load_rows(halo, F, s)
            here = tile(f, s, 0)
            flux = north_wind * (above + here) * 0.5
            for r in range(NR):
                at = pl.ds(pl.multiple_of(((f * S + s) * NR + r) * L, L), L)
                wind = jnp.concatenate([cy_ref[s, r], zeros], axis=1)
                zonal = jnp.concatenate([cx_ref[s, r], zeros], axis=1)
                after = tile(f, s, r + 1) if r < NR - 1 else below
                next_flux = wind * (here + after) * 0.5
                if r == NR - 1:
                    next_flux = next_flux * kept
                to_the_east = jnp.where(lane == W - 1, east_in[at, :], pltpu.roll(here, LANES - 1, 1))
                across = zonal * (here + to_the_east) * 0.5
                cw = west_in[pl.ds(1024 + (s * NR + r) * L, L), :]
                from_the_west = jnp.where(
                    lane == 0, cw * (west_in[at, :] + here) * 0.5, pltpu.roll(across, 1, 1))
                value = -((across - from_the_west) + (next_flux - flux))
                tend[pl.ds(pl.multiple_of(((s * F + f) * NR + r) * L, L), L), :] = jnp.where(lane < W, value, 0.0)
                flux, here = next_flux, after

    for k in range(2):
        upper = jnp.full((L, LANES), picks[k], jnp.int32) == k + 1

        @pl.loop(0, F)
        def _(f):
            for r in range(NR):
                low, high = [
                    tend[pl.ds(pl.multiple_of(((s * F + f) * NR + r) * L, L), L), :] for s in (k, k + 1)]
                rows_out[r, k, pl.ds(pl.multiple_of(f * L, L), L), :] = jnp.where(upper, high, low)

    def out_copy(k, i):
        to = (seat + i) % HALF
        return pltpu.make_async_remote_copy(
            rows_out.at[to, k], rows_in.at[seat, k], a_send.at[k, to], a_recv.at[k, seat],
            device_id={"lon": half * HALF + to}, device_id_type=MESH)

    def in_wait(k, i):
        source = (seat + HALF - i) % HALF
        pltpu.make_async_remote_copy(
            rows_out.at[source, k], rows_in.at[source, k], a_send.at[k, source], a_recv.at[k, source],
            device_id={"lon": half * HALF + source}, device_id_type=MESH).wait_recv()

    for k in range(2):
        for i in range(1, HALF):
            out_copy(k, i).start()
    rows_in[seat] = rows_out[seat]
    load_table.wait()

    def forward(k):
        for i in range(1, HALF):
            in_wait(k, i)
        total = jnp.zeros((F * L, 2 * KCUT), jnp.float32)
        for d in range(HALF):
            xh, xl = split2(rows_in[d, k])
            total += dot(xh, table[0, d], nn) + (dot(xl, table[0, d], nn) + dot(xh, table[1, d], nn))
        spec[k] = total

    def swap(k):
        return pltpu.make_async_remote_copy(
            spec.at[k], spec_in.at[k], y_send.at[k], y_recv.at[k], device_id={"lon": partner}, device_id_type=MESH)

    for k in range(2):
        forward(k)
        swap(k).start()

    wave = iota((F * L, 2 * KCUT), 1) % KCUT
    sign = jnp.where(wave % 2 == 0, 1.0, -1.0)
    scale = jnp.where(wave == 0, 1.0 / NLON, 2.0 / NLON)
    nt = ((1,), (1,))

    def back_copy(k, i):
        to = (seat + i) % HALF
        return pltpu.make_async_remote_copy(
            smooth_out.at[to, k], smooth_in.at[seat, k], b_send.at[k, to], b_recv.at[k, seat],
            device_id={"lon": half * HALF + to}, device_id_type=MESH)

    def back_wait(k, i):
        source = (seat + HALF - i) % HALF
        pltpu.make_async_remote_copy(
            smooth_out.at[source, k], smooth_in.at[source, k], b_send.at[k, source], b_recv.at[k, source],
            device_id={"lon": half * HALF + source}, device_id_type=MESH).wait_recv()

    for k in range(2):
        swap(k).wait()
        block = jnp.where(picks[k] == k + 1, blocks[k + 1], blocks[k])
        limit = cut_ref[block * NR + seat]
        kept = jnp.where(wave < jnp.full(wave.shape, limit, jnp.int32), scale, 0.0)
        xh, xl = split2((spec[k] + sign * spec_in[k]) * kept)
        for d in range(HALF):
            smooth_out[d, k] = dot(xh, table[0, d], nt) + (dot(xl, table[0, d], nt) + dot(xh, table[1, d], nt))
        for i in range(1, HALF):
            back_copy(k, i).start()
        smooth_in[seat, k] = smooth_out[seat, k]

    for k in range(2):
        for i in range(1, HALF):
            back_wait(k, i)

    for s in range(S):
        use = [
            jnp.full((L, LANES), jnp.where(picks[k] == s, polar[s], 0), jnp.int32) > 0
            for k in range(2)
        ]

        @pl.loop(0, F)
        def _(f):
            for r in range(NR):
                value = tend[pl.ds(pl.multiple_of(((s * F + f) * NR + r) * L, L), L), :]
                for k in range(2):
                    value = jnp.where(use[k], smooth_in[r, k, pl.ds(pl.multiple_of(f * L, L), L), :], value)
                out_ref[f, s, r] = value[:, :W]

    wait_pieces(s1, send1)
    wait_pieces(s2, send2)
    for k in range(2):
        for i in range(1, HALF):
            out_copy(k, i).wait_send()
            back_copy(k, i).wait_send()


def shards(table, state, courant_x, courant_y, block_of_slot, face_source, cutoff):
    vmem = pl.BlockSpec(memory_space=pltpu.VMEM)
    smem = pl.BlockSpec(memory_space=pltpu.SMEM)
    f32 = jnp.float32
    rows = F * S * NR * L
    dma = pltpu.SemaphoreType.DMA
    filtered = pl.pallas_call(
        step_kernel,
        out_shape=jax.ShapeDtypeStruct((F, S, NR, L, W), f32),
        in_specs=[smem, smem, smem, vmem, vmem, vmem, pl.BlockSpec(memory_space=pl.ANY)],
        out_specs=vmem,
        scratch_shapes=[
            pltpu.VMEM((2, HALF, LANES, 2 * KCUT), jnp.bfloat16),
            pltpu.VMEM((rows, LANES), f32),
            pltpu.VMEM((2 * PIECES, 128), f32),
            pltpu.VMEM((2 * PIECES, 128), f32),
            pltpu.VMEM((2 * PIECES, 128), f32),
            pltpu.VMEM((2 * PIECES, 128), f32),
            pltpu.VMEM((8, 1280), f32),
            pltpu.VMEM((8, 1280), f32),
            pltpu.VMEM((8, 1280), f32),
            pltpu.VMEM((1280, LANES), f32),
            pltpu.VMEM((1280, LANES), f32),
            pltpu.VMEM((rows, LANES), f32),
            pltpu.VMEM((NR, 2, F * L, LANES), f32),
            pltpu.VMEM((NR, 2, F * L, LANES), f32),
            pltpu.VMEM((2, F * L, 2 * KCUT), f32),
            pltpu.VMEM((2, F * L, 2 * KCUT), f32),
            pltpu.VMEM((NR, 2, F * L, LANES), f32),
            pltpu.VMEM((NR, 2, F * L, LANES), f32),
            dma, dma, dma, dma, dma,
            dma((2,)), dma((2,)),
            dma((2, HALF)), dma((2, HALF)),
            dma((2,)), dma((2,)),
            dma((2, HALF)), dma((2, HALF)),
        ],
        compiler_params=pltpu.CompilerParams(
            collective_id=0, has_side_effects=True, vmem_limit_bytes=48 << 20),
    )(block_of_slot, face_source, cutoff, state, courant_x, courant_y, table)
    return state + filtered


def solution(mesh):
    placed = (
        P(),
        P(None, "lat", None, None, "lon"),
        P("lat", None, None, "lon"),
        P("lat", None, None, "lon"),
        P("lat"),
        P("lat", None),
        P(),
    )
    body = jax.shard_map(
        shards,
        mesh=mesh,
        in_specs=placed,
        out_specs=P(None, "lat", None, None, "lon"),
        check_vma=False,
    )
    table = basis_table()
    return lambda *arrays: body(jnp.asarray(table), *arrays)
```

```python
import math

import jax
import jax.numpy as jnp
import numpy as np
from jax import lax
from jax.experimental import pallas as pl
from jax.experimental.pallas import tpu as pltpu
from jax.sharding import PartitionSpec as P

NLON = 2880
KCUT = 256
F, S, NR, L, W = 5, 3, 8, 8, 180
NBLK, POLAR = 144, 24
LANES = 256
NLAT, NLONDEV, HALF = 48, 16, 8
PIECES = NLAT * 8
MESH = pl.DeviceIdType.MESH
HIGHEST = lax.Precision.HIGHEST


def basis_table():
    column = np.arange(HALF * W, dtype=np.int64)
    phase = ((column[:, None] * np.arange(KCUT)[None, :]) % NLON) * (2.0 * math.pi / NLON)
    table = np.concatenate([np.cos(phase), np.sin(phase)], axis=1).reshape(HALF, W, 2 * KCUT)
    table = np.pad(table, ((0, 0), (0, LANES - W), (0, 0))).astype(np.float32)
    high = table.astype(jnp.bfloat16)
    low = (table - high.astype(np.float32)).astype(jnp.bfloat16)
    return np.stack([high, low])


def split2(x):
    high = x.astype(jnp.bfloat16)
    return high, (x - high.astype(jnp.float32)).astype(jnp.bfloat16)


def split3(x):
    high = x.astype(jnp.bfloat16)
    rest = x - high.astype(jnp.float32)
    mid = rest.astype(jnp.bfloat16)
    return high, mid, (rest - mid.astype(jnp.float32)).astype(jnp.bfloat16)


def dot(a, b, dims):
    return lax.dot_general(a, b, (dims, ((), ())), preferred_element_type=jnp.float32)


def store_rows(main, tail, c, t, value):
    main[pl.ds(c * 64 + t, L, stride=8), :] = value[:, :128]
    tail[pl.ds(c * 64 + t, L, stride=8), :] = value[:, 128:]


def load_rows(main, tail, c, t):
    at = pl.ds(c * 64 + t, L, stride=8)
    return jnp.concatenate([main[at, :], tail[at, :]], axis=1)


def pack(main, tail):
    shape = (NLAT, 8, 128)
    main, tail = main.reshape(shape), tail.reshape(shape)
    sub, lane = iota(shape, 1), iota(shape, 2)
    pairs = jnp.where(lane < 64, tail, pltpu.roll(pltpu.roll(tail, 5, 1), 64, 2))
    first = jnp.where(sub < 6, main, pltpu.roll(pairs, 6, 1))
    return jnp.stack([first, pltpu.roll(pairs, 6, 1)], axis=1).reshape(2 * PIECES, 128)


def unpack(packed):
    shape = (NLAT, 8, 128)
    sub = iota(shape, 1)
    packed = packed.reshape(NLAT, 2, 8, 128)
    first, second = packed[:, 0], packed[:, 1]
    pairs = jnp.where(sub < 2, pltpu.roll(first, 2, 1), pltpu.roll(second, 2, 1))
    tail = jnp.where(sub < 3, pairs, pltpu.roll(pltpu.roll(pairs, 3, 1), 64, 2))
    keep = sub < 6
    main, tail = jnp.where(keep, first, 0.0), jnp.where(keep, tail, 0.0)
    return main.reshape(PIECES, 128), tail.reshape(PIECES, 128)


def iota(shape, dim):
    return lax.broadcasted_iota(jnp.int32, shape, dim)


def step_kernel(
    block_in, face_in, cut_in, state_in, cx_in, cy_in, table_hbm,
    out_ref,
    block_ref, face_ref, cut_ref, state_ref, cx_ref, cy_ref,
    table, padded, main, tail, send1, got1, send2, halo,
    edges, from_west, from_east, east_in, west_in,
    tend, rows_out, rows_in, spec, spec_in, smooth_out, smooth_in,
    load_sem, table_sem, s1, r1, s2, r2, edge_send, edge_recv, a_send, a_recv, y_send, y_recv, b_send, b_recv,
):
    lat, lon = lax.axis_index("lat"), lax.axis_index("lon")
    half, seat = lon // HALF, lon % HALF
    partner = (lon + HALF) % NLONDEV
    east, west = (lon + 1) % NLONDEV, (lon + NLONDEV - 1) % NLONDEV

    loads = [
        pltpu.make_async_copy(source, target, load_sem.at[i])
        for i, (source, target) in enumerate([
            (state_in, state_ref), (cy_in, cy_ref), (face_in, face_ref),
            (block_in, block_ref), (cx_in, cx_ref), (cut_in, cut_ref)])
    ]
    for load in loads:
        load.start()
    load_table = pltpu.make_async_copy(table_hbm, table, table_sem)
    load_table.start()
    main[...] = jnp.zeros_like(main)
    tail[...] = jnp.zeros_like(tail)
    padded[...] = jnp.zeros_like(padded)
    edges[...] = jnp.zeros_like(edges)
    for load in loads:
        load.wait()

    blocks = [block_ref[s] for s in range(S)]
    polar = [jnp.where(b < POLAR, 1, 0) + jnp.where(b >= NBLK - POLAR, 1, 0) for b in blocks]
    cols, keep = [], []
    for t in range(2 * S):
        n = face_ref[t // S, t % S]
        safe = jnp.maximum(n, 0)
        cols.append(jnp.where(n >= 0, 8 * lax.div(safe, S) + lax.rem(safe, S) + (t // S) * S, -1))
        keep.append(jnp.where(n >= 0, 1.0, 0.0))
    keep = keep[S:]
    first = (1 - polar[0]) * polar[2]
    picks = [first, 1 + polar[2]]

    lane = iota((L, LANES), 1)

    padded[:, :W] = state_ref[...].reshape(F * S * NR * L, W)

    def tile(f, s, r):
        return padded[pl.ds(pl.multiple_of(((f * S + s) * NR + r) * L, L), L), :]

    for t in range(2 * S):
        s = t % S
        want = jnp.full((L, LANES), cols[t].astype(jnp.float32), jnp.float32)
        for f in range(F):
            row = tile(f, s, NR - 1 if t < S else 0)
            store_rows(main, tail, f, t, jnp.where(lane == W, want, row))
        if t < S:
            wind = jnp.concatenate([cy_ref[s, NR - 1], jnp.zeros((L, LANES - W), jnp.float32)], axis=1)
            store_rows(main, tail, F, t, jnp.where(lane == W, want, wind))
        else:
            store_rows(main, tail, F, t, jnp.where(lane == W, want, 0.0))

    send1[...] = pack(main[...], tail[...])

    pick = jnp.where(
        jnp.logical_or(
            jnp.logical_and(iota((8, W), 0) == 0, iota((8, W), 1) == 0),
            jnp.logical_and(iota((8, W), 0) == 1, iota((8, W), 1) == W - 1),
        ),
        1.0, 0.0,
    ).astype(jnp.float32)
    edges[:, :960] = lax.dot_general(
        pick, state_ref[...].reshape(F * S * NR * L, W), (((1,), (1,)), ((), ())),
        precision=HIGHEST, preferred_element_type=jnp.float32)
    edges[:, 1024:1216] = lax.dot_general(
        pick, cx_ref[...].reshape(S * NR * L, W), (((1,), (1,)), ((), ())),
        precision=HIGHEST, preferred_element_type=jnp.float32)

    def piece(ref, i):
        return ref.at[pl.ds(pl.multiple_of(i * 16, 16), 9), :]

    @pl.loop(1, NLAT)
    def _(i):
        to = (lat + i) % NLAT
        pltpu.make_async_remote_copy(
            piece(send1, to), piece(got1, lat), s1, r1, device_id={"lat": to}, device_id_type=MESH).start()

    to_west = pltpu.make_async_remote_copy(
        edges, from_east, edge_send.at[0], edge_recv.at[0], device_id={"lon": west}, device_id_type=MESH)
    to_east = pltpu.make_async_remote_copy(
        edges, from_west, edge_send.at[1], edge_recv.at[1], device_id={"lon": east}, device_id_type=MESH)
    to_west.start()
    to_east.start()
    mine = pl.ds(pl.multiple_of(lat * 16, 16), 16)
    got1[mine, :] = send1[mine, :]

    def wait_pieces(sem, ref):
        whole = ref.at[pl.ds(0, 9 * (NLAT - 1)), :]
        pltpu.make_async_copy(whole, whole, sem).wait()

    wait_pieces(r1, got1)
    pieces = jnp.concatenate(unpack(got1[...]), axis=1)
    asked = jnp.broadcast_to(pieces[:, W:W + 1], (PIECES, PIECES))
    onehot = jnp.where(asked == iota((PIECES, PIECES), 1).astype(jnp.float32), 1.0, 0.0).astype(jnp.bfloat16)
    a, b, c = split3(pieces)
    nn = ((1,), (0,))
    found = (dot(onehot, a, nn) + dot(onehot, b, nn)) + dot(onehot, c, nn)
    send2[...] = pack(found[:, :128], found[:, 128:])

    @pl.loop(1, NLAT)
    def _(i):
        to = (lat + i) % NLAT
        pltpu.make_async_remote_copy(
            piece(send2, to), piece(halo, lat), s2, r2, device_id={"lat": to}, device_id_type=MESH).start()

    halo[mine, :] = send2[mine, :]

    to_west.wait()
    to_east.wait()
    place = lambda src, dst: jnp.where(
        jnp.logical_and(iota((8, LANES), 0) == src, iota((8, LANES), 1) == dst), 1.0, 0.0).astype(jnp.float32)
    tn = (((0,), (0,)), ((), ()))
    east_in[...] = lax.dot_general(
        from_east[...], place(0, W - 1), tn, precision=HIGHEST, preferred_element_type=jnp.float32)
    west_in[...] = lax.dot_general(
        from_west[...], place(1, 0), tn, precision=HIGHEST, preferred_element_type=jnp.float32)
    wait_pieces(r2, halo)
    main[...], tail[...] = unpack(halo[...])

    zeros = jnp.zeros((L, LANES - W), jnp.float32)

    for s in range(S):
        kept = jnp.full((L, LANES), keep[s], jnp.float32)

        @pl.loop(0, F)
        def _(f):
            above, below = load_rows(main, tail, f, s), load_rows(main, tail, f, S + s)
            north_wind = load_rows(main, tail, F, s)
            here = tile(f, s, 0)
            flux = north_wind * (above + here) * 0.5
            for r in range(NR):
                at = pl.ds(pl.multiple_of(((f * S + s) * NR + r) * L, L), L)
                wind = jnp.concatenate([cy_ref[s, r], zeros], axis=1)
                zonal = jnp.concatenate([cx_ref[s, r], zeros], axis=1)
                after = tile(f, s, r + 1) if r < NR - 1 else below
                next_flux = wind * (here + after) * 0.5
                if r == NR - 1:
                    next_flux = next_flux * kept
                to_the_east = jnp.where(lane == W - 1, east_in[at, :], pltpu.roll(here, LANES - 1, 1))
                across = zonal * (here + to_the_east) * 0.5
                cw = west_in[pl.ds(1024 + (s * NR + r) * L, L), :]
                from_the_west = jnp.where(
                    lane == 0, cw * (west_in[at, :] + here) * 0.5, pltpu.roll(across, 1, 1))
                value = -((across - from_the_west) + (next_flux - flux))
                tend[pl.ds(pl.multiple_of(((s * F + f) * NR + r) * L, L), L), :] = jnp.where(lane < W, value, 0.0)
                flux, here = next_flux, after

    for k in range(2):
        upper = jnp.full((L, LANES), picks[k], jnp.int32) == k + 1

        @pl.loop(0, F)
        def _(f):
            for r in range(NR):
                low, high = [
                    tend[pl.ds(pl.multiple_of(((s * F + f) * NR + r) * L, L), L), :] for s in (k, k + 1)]
                rows_out[r, k, pl.ds(pl.multiple_of(f * L, L), L), :] = jnp.where(upper, high, low)

    def out_copy(k, i):
        to = (seat + i) % HALF
        return pltpu.make_async_remote_copy(
            rows_out.at[to, k], rows_in.at[seat, k], a_send.at[k, to], a_recv.at[k, seat],
            device_id={"lon": half * HALF + to}, device_id_type=MESH)

    def in_wait(k, i):
        source = (seat + HALF - i) % HALF
        pltpu.make_async_remote_copy(
            rows_out.at[source, k], rows_in.at[source, k], a_send.at[k, source], a_recv.at[k, source],
            device_id={"lon": half * HALF + source}, device_id_type=MESH).wait_recv()

    for k in range(2):
        for i in range(1, HALF):
            out_copy(k, i).start()
    rows_in[seat] = rows_out[seat]
    load_table.wait()

    def forward(k):
        for i in range(1, HALF):
            in_wait(k, i)
        total = jnp.zeros((F * L, 2 * KCUT), jnp.float32)
        for d in range(HALF):
            xh, xl = split2(rows_in[d, k])
            total += dot(xh, table[0, d], nn) + (dot(xl, table[0, d], nn) + dot(xh, table[1, d], nn))
        spec[k] = total

    def swap(k):
        return pltpu.make_async_remote_copy(
            spec.at[k], spec_in.at[k], y_send.at[k], y_recv.at[k], device_id={"lon": partner}, device_id_type=MESH)

    for k in range(2):
        forward(k)
        swap(k).start()

    wave = iota((F * L, 2 * KCUT), 1) % KCUT
    sign = jnp.where(wave % 2 == 0, 1.0, -1.0)
    scale = jnp.where(wave == 0, 1.0 / NLON, 2.0 / NLON)
    nt = ((1,), (1,))

    def back_copy(k, i):
        to = (seat + i) % HALF
        return pltpu.make_async_remote_copy(
            smooth_out.at[to, k], smooth_in.at[seat, k], b_send.at[k, to], b_recv.at[k, seat],
            device_id={"lon": half * HALF + to}, device_id_type=MESH)

    def back_wait(k, i):
        source = (seat + HALF - i) % HALF
        pltpu.make_async_remote_copy(
            smooth_out.at[source, k], smooth_in.at[source, k], b_send.at[k, source], b_recv.at[k, source],
            device_id={"lon": half * HALF + source}, device_id_type=MESH).wait_recv()

    for k in range(2):
        swap(k).wait()
        block = jnp.where(picks[k] == k + 1, blocks[k + 1], blocks[k])
        limit = cut_ref[block * NR + seat]
        kept = jnp.where(wave < jnp.full(wave.shape, limit, jnp.int32), scale, 0.0)
        xh, xl = split2((spec[k] + sign * spec_in[k]) * kept)
        for d in range(HALF):
            smooth_out[d, k] = dot(xh, table[0, d], nt) + (dot(xl, table[0, d], nt) + dot(xh, table[1, d], nt))
        for i in range(1, HALF):
            back_copy(k, i).start()
        smooth_in[seat, k] = smooth_out[seat, k]

    for k in range(2):
        for i in range(1, HALF):
            back_wait(k, i)

    for s in range(S):
        use = [
            jnp.full((L, LANES), jnp.where(picks[k] == s, polar[s], 0), jnp.int32) > 0
            for k in range(2)
        ]

        @pl.loop(0, F)
        def _(f):
            for r in range(NR):
                value = tend[pl.ds(pl.multiple_of(((s * F + f) * NR + r) * L, L), L), :]
                for k in range(2):
                    value = jnp.where(use[k], smooth_in[r, k, pl.ds(pl.multiple_of(f * L, L), L), :], value)
                out_ref[f, s, r] = value[:, :W]

    wait_pieces(s1, send1)
    wait_pieces(s2, send2)
    for k in range(2):
        for i in range(1, HALF):
            out_copy(k, i).wait_send()
            back_copy(k, i).wait_send()


def shards(table, state, courant_x, courant_y, block_of_slot, face_source, cutoff):
    vmem = pl.BlockSpec(memory_space=pltpu.VMEM)
    i32 = jnp.int32
    f32 = jnp.float32
    rows = F * S * NR * L
    dma = pltpu.SemaphoreType.DMA
    filtered = pl.pallas_call(
        step_kernel,
        out_shape=jax.ShapeDtypeStruct((F, S, NR, L, W), f32),
        in_specs=[pl.BlockSpec(memory_space=pltpu.HBM)] * 7,
        out_specs=vmem,
        scratch_shapes=[
            pltpu.SMEM((S,), i32),
            pltpu.SMEM((2, S), i32),
            pltpu.SMEM((NBLK * NR,), i32),
            pltpu.VMEM((F, S, NR, L, W), f32),
            pltpu.VMEM((S, NR, L, W), f32),
            pltpu.VMEM((S, NR, L, W), f32),
            pltpu.VMEM((2, HALF, LANES, 2 * KCUT), jnp.bfloat16),
            pltpu.VMEM((rows, LANES), f32),
            pltpu.VMEM((PIECES, 128), f32),
            pltpu.VMEM((PIECES, 128), f32),
            pltpu.VMEM((2 * PIECES, 128), f32),
            pltpu.VMEM((2 * PIECES, 128), f32),
            pltpu.VMEM((2 * PIECES, 128), f32),
            pltpu.VMEM((2 * PIECES, 128), f32),
            pltpu.VMEM((8, 1280), f32),
            pltpu.VMEM((8, 1280), f32),
            pltpu.VMEM((8, 1280), f32),
            pltpu.VMEM((1280, LANES), f32),
            pltpu.VMEM((1280, LANES), f32),
            pltpu.VMEM((rows, LANES), f32),
            pltpu.VMEM((NR, 2, F * L, LANES), f32),
            pltpu.VMEM((NR, 2, F * L, LANES), f32),
            pltpu.VMEM((2, F * L, 2 * KCUT), f32),
            pltpu.VMEM((2, F * L, 2 * KCUT), f32),
            pltpu.VMEM((NR, 2, F * L, LANES), f32),
            pltpu.VMEM((NR, 2, F * L, LANES), f32),
            dma((6,)), dma, dma, dma, dma, dma,
            dma((2,)), dma((2,)),
            dma((2, HALF)), dma((2, HALF)),
            dma((2,)), dma((2,)),
            dma((2, HALF)), dma((2, HALF)),
        ],
        compiler_params=pltpu.CompilerParams(
            has_side_effects=True, vmem_limit_bytes=48 << 20),
    )(block_of_slot, face_source.T, cutoff, state, courant_x, courant_y, table)
    return state + filtered


def solution(mesh):
    placed = (
        P(),
        P(None, "lat", None, None, "lon"),
        P("lat", None, None, "lon"),
        P("lat", None, None, "lon"),
        P("lat"),
        P("lat", None),
        P(),
    )
    body = jax.shard_map(
        shards,
        mesh=mesh,
        in_specs=placed,
        out_specs=P(None, "lat", None, None, "lon"),
        check_vma=False,
    )
    table = basis_table()
    return lambda *arrays: body(jnp.asarray(table), *arrays)
```

```python
import math

import jax
import jax.numpy as jnp
import numpy as np
from jax import lax
from jax.experimental import pallas as pl
from jax.experimental.pallas import tpu as pltpu
from jax.sharding import PartitionSpec as P

NLON = 2880
KCUT = 256
F, S, NR, L, W = 5, 3, 8, 8, 180
NBLK, POLAR = 144, 24
LANES = 256
NLAT, NLONDEV, HALF = 48, 16, 8
PIECES = NLAT * 8
INNER, ROWS = 64, 88
MESH = pl.DeviceIdType.MESH
HIGHEST = lax.Precision.HIGHEST


def basis_table():
    column = np.arange(HALF * W, dtype=np.int64)
    phase = ((column[:, None] * np.arange(KCUT)[None, :]) % NLON) * (2.0 * math.pi / NLON)
    table = np.concatenate([np.cos(phase), np.sin(phase)], axis=1).reshape(HALF, W, 2 * KCUT)
    table = np.pad(table, ((0, 0), (0, LANES - W), (0, 0))).astype(np.float32)
    high = table.astype(jnp.bfloat16)
    low = (table - high.astype(np.float32)).astype(jnp.bfloat16)
    return np.stack([high, low])


def split2(x):
    high = x.astype(jnp.bfloat16)
    return high, (x - high.astype(jnp.float32)).astype(jnp.bfloat16)


def split3(x):
    high = x.astype(jnp.bfloat16)
    rest = x - high.astype(jnp.float32)
    mid = rest.astype(jnp.bfloat16)
    return high, mid, (rest - mid.astype(jnp.float32)).astype(jnp.bfloat16)


def dot(a, b, dims):
    return lax.dot_general(a, b, (dims, ((), ())), preferred_element_type=jnp.float32)


def store_rows(main, tail, c, t, value):
    main[pl.ds(c * 64 + t, L, stride=8), :] = value[:, :128]
    tail[pl.ds(c * 64 + t, L, stride=8), :] = value[:, 128:]


def load_rows(main, tail, c, t):
    at = pl.ds(c * 64 + t, L, stride=8)
    return jnp.concatenate([main[at, :], tail[at, :]], axis=1)


def pack(main, tail):
    shape = (NLAT, 8, 128)
    main, tail = main.reshape(shape), tail.reshape(shape)
    sub, lane = iota(shape, 1), iota(shape, 2)
    pairs = jnp.where(lane < 64, tail, pltpu.roll(pltpu.roll(tail, 5, 1), 64, 2))
    first = jnp.where(sub < 6, main, pltpu.roll(pairs, 6, 1))
    return jnp.stack([first, pltpu.roll(pairs, 6, 1)], axis=1).reshape(2 * PIECES, 128)


def unpack(packed):
    shape = (NLAT, 8, 128)
    sub = iota(shape, 1)
    packed = packed.reshape(NLAT, 2, 8, 128)
    first, second = packed[:, 0], packed[:, 1]
    pairs = jnp.where(sub < 2, pltpu.roll(first, 2, 1), pltpu.roll(second, 2, 1))
    tail = jnp.where(sub < 3, pairs, pltpu.roll(pltpu.roll(pairs, 3, 1), 64, 2))
    keep = sub < 6
    main, tail = jnp.where(keep, first, 0.0), jnp.where(keep, tail, 0.0)
    return main.reshape(PIECES, 128), tail.reshape(PIECES, 128)


def iota(shape, dim):
    return lax.broadcasted_iota(jnp.int32, shape, dim)


def step_kernel(
    block_in, face_in, cut_in, state_in, cx_in, cy_in, table_hbm,
    out_ref,
    block_ref, face_ref, cut_ref, state_ref, cx_ref, cy_ref,
    table, padded, main, tail, send1, got1, send2, halo,
    edges, from_west, from_east, east_in, west_in,
    tend, rows_out, rows_in, spec, spec_in, smooth_out, smooth_in,
    load_sem, table_sem, s1, r1, s2, r2, edge_send, edge_recv, a_send, a_recv, y_send, y_recv, b_send, b_recv,
):
    lat, lon = lax.axis_index("lat"), lax.axis_index("lon")
    half, seat = lon // HALF, lon % HALF
    partner = (lon + HALF) % NLONDEV
    east, west = (lon + 1) % NLONDEV, (lon + NLONDEV - 1) % NLONDEV

    barrier = pltpu.get_barrier_semaphore()

    @pl.loop(1, NLAT)
    def _(i):
        pl.semaphore_signal(barrier, inc=1, device_id={"lat": (lat + i) % NLAT}, device_id_type=MESH)

    @pl.loop(1, NLONDEV)
    def _(i):
        pl.semaphore_signal(barrier, inc=1, device_id={"lon": (lon + i) % NLONDEV}, device_id_type=MESH)

    loads = [
        pltpu.make_async_copy(source, target, load_sem.at[i])
        for i, (source, target) in enumerate([
            (state_in, state_ref), (cy_in, cy_ref), (face_in, face_ref),
            (block_in, block_ref), (cx_in, cx_ref), (cut_in, cut_ref)])
    ]
    for load in loads:
        load.start()
    load_table = pltpu.make_async_copy(table_hbm, table, table_sem)
    load_table.start()
    main[...] = jnp.zeros_like(main)
    tail[...] = jnp.zeros_like(tail)
    padded[...] = jnp.zeros_like(padded)
    edges[...] = jnp.zeros_like(edges)
    for load in loads:
        load.wait()

    blocks = [block_ref[s] for s in range(S)]
    polar = [jnp.where(b < POLAR, 1, 0) + jnp.where(b >= NBLK - POLAR, 1, 0) for b in blocks]
    cols, keep = [], []
    for t in range(2 * S):
        n = face_ref[t // S, t % S]
        safe = jnp.maximum(n, 0)
        cols.append(jnp.where(n >= 0, 8 * lax.div(safe, S) + lax.rem(safe, S) + (t // S) * S, -1))
        keep.append(jnp.where(n >= 0, 1.0, 0.0))
    keep = keep[S:]
    first = (1 - polar[0]) * polar[2]
    picks = [first, 1 + polar[2]]

    lane = iota((L, LANES), 1)

    padded[:, :W] = state_ref[...].reshape(F * S * NR * L, W)

    def tile(f, s, r):
        return padded[pl.ds(pl.multiple_of(((f * S + s) * NR + r) * L, L), L), :]

    for t in range(2 * S):
        s = t % S
        want = jnp.full((L, LANES), cols[t].astype(jnp.float32), jnp.float32)
        for f in range(F):
            row = tile(f, s, NR - 1 if t < S else 0)
            store_rows(main, tail, f, t, jnp.where(lane == W, want, row))
        if t < S:
            wind = jnp.concatenate([cy_ref[s, NR - 1], jnp.zeros((L, LANES - W), jnp.float32)], axis=1)
            store_rows(main, tail, F, t, jnp.where(lane == W, want, wind))
        else:
            store_rows(main, tail, F, t, jnp.where(lane == W, want, 0.0))

    send1[...] = pack(main[...], tail[...])

    pick = jnp.where(
        jnp.logical_or(
            jnp.logical_and(iota((8, W), 0) == 0, iota((8, W), 1) == 0),
            jnp.logical_and(iota((8, W), 0) == 1, iota((8, W), 1) == W - 1),
        ),
        1.0, 0.0,
    ).astype(jnp.float32)
    edges[:, :960] = lax.dot_general(
        pick, state_ref[...].reshape(F * S * NR * L, W), (((1,), (1,)), ((), ())),
        precision=HIGHEST, preferred_element_type=jnp.float32)
    edges[:, 1024:1216] = lax.dot_general(
        pick, cx_ref[...].reshape(S * NR * L, W), (((1,), (1,)), ((), ())),
        precision=HIGHEST, preferred_element_type=jnp.float32)

    rows_out[...] = jnp.zeros_like(rows_out)
    pl.semaphore_wait(barrier, NLAT - 1 + NLONDEV - 1)

    to_west = pltpu.make_async_remote_copy(
        edges, from_east, edge_send.at[0], edge_recv.at[0], device_id={"lon": west}, device_id_type=MESH)
    to_east = pltpu.make_async_remote_copy(
        edges, from_west, edge_send.at[1], edge_recv.at[1], device_id={"lon": east}, device_id_type=MESH)
    to_west.start()
    to_east.start()

    def piece(ref, i):
        return ref.at[pl.ds(pl.multiple_of(i * 16, 16), 9), :]

    def send_pieces(source, target, send_sem, recv_sem):
        @pl.loop(1, NLAT)
        def _(i):
            to = (lat + i) % NLAT
            pltpu.make_async_remote_copy(
                piece(source, to), piece(target, lat), send_sem, recv_sem,
                device_id={"lat": to}, device_id_type=MESH).start()

    def wait_pieces(sem, ref):
        whole = ref.at[pl.ds(0, 9 * (NLAT - 1)), :]
        pltpu.make_async_copy(whole, whole, sem).wait()

    mine = pl.ds(pl.multiple_of(lat * 16, 16), 16)
    send_pieces(send1, got1, s1, r1)
    got1[mine, :] = send1[mine, :]

    to_west.wait()
    to_east.wait()
    place = lambda src, dst: jnp.where(
        jnp.logical_and(iota((8, LANES), 0) == src, iota((8, LANES), 1) == dst), 1.0, 0.0).astype(jnp.float32)
    tn = (((0,), (0,)), ((), ()))
    east_in[...] = lax.dot_general(
        from_east[...], place(0, W - 1), tn, precision=HIGHEST, preferred_element_type=jnp.float32)
    west_in[...] = lax.dot_general(
        from_west[...], place(1, 0), tn, precision=HIGHEST, preferred_element_type=jnp.float32)

    zeros = jnp.zeros((L, LANES - W), jnp.float32)

    def at_row(f, s, r):
        return pl.ds(pl.multiple_of(((f * S + s) * NR + r) * L, L), L)

    def tend_row(f, s, r):
        return pl.ds(pl.multiple_of(((s * F + f) * NR + r) * L, L), L)

    def put_tendency(f, s, r, here, merid):
        at = at_row(f, s, r)
        zonal = jnp.concatenate([cx_ref[s, r], zeros], axis=1)
        to_the_east = jnp.where(lane == W - 1, east_in[at, :], pltpu.roll(here, LANES - 1, 1))
        across = zonal * (here + to_the_east) * 0.5
        cw = west_in[pl.ds(1024 + (s * NR + r) * L, L), :]
        from_the_west = jnp.where(lane == 0, cw * (west_in[at, :] + here) * 0.5, pltpu.roll(across, 1, 1))
        tend[tend_row(f, s, r), :] = jnp.where(lane < W, -((across - from_the_west) + merid), 0.0)

    def wind(s, r):
        return jnp.concatenate([cy_ref[s, r], zeros], axis=1)

    for s in range(S):
        @pl.loop(0, F)
        def _(f):
            here = tile(f, s, 1)
            flux = wind(s, 0) * (tile(f, s, 0) + here) * 0.5
            for r in range(1, NR - 1):
                after = tile(f, s, r + 1)
                next_flux = wind(s, r) * (here + after) * 0.5
                put_tendency(f, s, r, here, next_flux - flux)
                flux, here = next_flux, after

    def spot(r, k, f):
        if 0 < r < NR - 1:
            n = ((r - 1) * 2 + k) * F + f
            return (n // 8) * ROWS + (n % 8) * L
        n = ((r // (NR - 1)) * 2 + k) * F + f
        return (n // 3) * ROWS + INNER + (n % 3) * L

    def spot_rows(r, k, f):
        return pl.ds(pl.multiple_of(spot(r, k, f), L), L)

    uppers = [jnp.full((L, LANES), picks[k], jnp.int32) == k + 1 for k in range(2)]

    def gather_rows(rs):
        for k in range(2):
            @pl.loop(0, F)
            def _(f):
                for r in rs:
                    low, high = tend[tend_row(f, k, r), :], tend[tend_row(f, k + 1, r), :]
                    rows_out[spot_rows(r, k, f), :] = jnp.where(uppers[k], high, low)

    starts, sizes = (0, INNER), (INNER, ROWS - INNER)

    def part(g, i):
        return pl.ds(pl.multiple_of(i * ROWS + starts[g], L), sizes[g])

    def seat_copy(g, i, source, target, send_sem, recv_sem):
        to = (seat + i) % HALF
        return pltpu.make_async_remote_copy(
            source.at[part(g, to), :], target.at[part(g, seat), :], send_sem.at[g, to], recv_sem.at[g, seat],
            device_id={"lon": half * HALF + to}, device_id_type=MESH)

    def seat_wait(g, i, source, target, send_sem, recv_sem):
        other = (seat + HALF - i) % HALF
        pltpu.make_async_remote_copy(
            source.at[part(g, other), :], target.at[part(g, other), :], send_sem.at[g, other],
            recv_sem.at[g, other], device_id={"lon": half * HALF + other}, device_id_type=MESH).wait_recv()

    there = (rows_out, rows_in, a_send, a_recv)
    back = (smooth_out, smooth_in, b_send, b_recv)

    def exchange(g, way):
        for i in range(1, HALF):
            seat_copy(g, i, *way).start()
        way[1][part(g, seat), :] = way[0][part(g, seat), :]

    def arrive(g, way):
        for i in range(1, HALF):
            seat_wait(g, i, *way)

    def leave(g, way):
        for i in range(1, HALF):
            seat_copy(g, i, *way).wait_send()

    nn, nt = ((1,), (0,)), ((1,), (1,))

    def forward(g):
        total = jnp.zeros((sizes[g], 2 * KCUT), jnp.float32)
        for d in range(HALF):
            xh, xl = split2(rows_in[d * ROWS + starts[g]:d * ROWS + starts[g] + sizes[g], :])
            total += dot(xh, table[0, d], nn) + (dot(xl, table[0, d], nn) + dot(xh, table[1, d], nn))
        spec[starts[g]:starts[g] + sizes[g], :] = total

    def swap(g):
        rows = pl.ds(starts[g], sizes[g])
        return pltpu.make_async_remote_copy(
            spec.at[rows, :], spec_in.at[rows, :], y_send.at[g], y_recv.at[g],
            device_id={"lon": partner}, device_id_type=MESH)

    chosen = [jnp.where(picks[k] == k + 1, blocks[k + 1], blocks[k]) for k in range(2)]

    def limits(g):
        parts = []
        for j in range(sizes[g] // L):
            if g == 0:
                n = seat * 8 + j
                r = 1 + n // (2 * F)
            else:
                n = seat * 3 + j
                r = jnp.minimum(n // (2 * F), 1) * (NR - 1)
            block = jnp.where((n // F) % 2 == 0, chosen[0], chosen[1])
            parts.append(jnp.full((L, 2 * KCUT), cut_ref[block * NR + r], jnp.int32))
        return jnp.concatenate(parts, axis=0)

    def inverse(g):
        shape = (sizes[g], 2 * KCUT)
        wave = iota(shape, 1) % KCUT
        sign = jnp.where(wave % 2 == 0, 1.0, -1.0)
        scale = jnp.where(wave == 0, 1.0 / NLON, 2.0 / NLON)
        rows = slice(starts[g], starts[g] + sizes[g])
        weights = jnp.where(wave < limits(g), scale, 0.0)
        xh, xl = split2((spec[rows, :] + sign * spec_in[rows, :]) * weights)
        for d in range(HALF):
            smooth_out[d * ROWS + starts[g]:d * ROWS + starts[g] + sizes[g], :] = dot(xh, table[0, d], nt) + (
                dot(xl, table[0, d], nt) + dot(xh, table[1, d], nt))

    gather_rows(range(1, NR - 1))
    exchange(0, there)

    wait_pieces(r1, got1)
    pieces = jnp.concatenate(unpack(got1[...]), axis=1)
    asked = jnp.broadcast_to(pieces[:, W:W + 1], (PIECES, PIECES))
    onehot = jnp.where(asked == iota((PIECES, PIECES), 1).astype(jnp.float32), 1.0, 0.0).astype(jnp.bfloat16)
    a, b, c = split3(pieces)
    found = (dot(onehot, a, nn) + dot(onehot, b, nn)) + dot(onehot, c, nn)
    send2[...] = pack(found[:, :128], found[:, 128:])
    send_pieces(send2, halo, s2, r2)
    halo[mine, :] = send2[mine, :]

    load_table.wait()
    arrive(0, there)
    forward(0)
    swap(0).start()

    wait_pieces(r2, halo)
    main[...], tail[...] = unpack(halo[...])
    for s in range(S):
        kept = jnp.full((L, LANES), keep[s], jnp.float32)

        @pl.loop(0, F)
        def _(f):
            above, below = load_rows(main, tail, f, s), load_rows(main, tail, f, S + s)
            north_wind = load_rows(main, tail, F, s)
            here, after = tile(f, s, 0), tile(f, s, 1)
            put_tendency(
                f, s, 0, here, wind(s, 0) * (here + after) * 0.5 - north_wind * (above + here) * 0.5)
            before, here = tile(f, s, NR - 2), tile(f, s, NR - 1)
            put_tendency(
                f, s, NR - 1, here,
                wind(s, NR - 1) * (here + below) * 0.5 * kept - wind(s, NR - 2) * (before + here) * 0.5)

    gather_rows((0, NR - 1))
    exchange(1, there)

    swap(0).wait()
    inverse(0)
    exchange(0, back)

    arrive(1, there)
    forward(1)
    swap(1).start()
    swap(1).wait()
    inverse(1)
    exchange(1, back)

    uses = [
        [jnp.full((L, LANES), jnp.where(picks[k] == s, polar[s], 0), jnp.int32) > 0 for k in range(2)]
        for s in range(S)
    ]

    def finish(rs):
        for s in range(S):
            @pl.loop(0, F)
            def _(f):
                for r in rs:
                    value = tend[tend_row(f, s, r), :]
                    for k in range(2):
                        value = jnp.where(uses[s][k], smooth_in[spot_rows(r, k, f), :], value)
                    out_ref[f, s, r] = value[:, :W]

    arrive(0, back)
    finish(range(1, NR - 1))
    arrive(1, back)
    finish((0, NR - 1))

    wait_pieces(s1, send1)
    wait_pieces(s2, send2)
    for g in range(2):
        leave(g, there)
        leave(g, back)


def shards(table, state, courant_x, courant_y, block_of_slot, face_source, cutoff):
    vmem = pl.BlockSpec(memory_space=pltpu.VMEM)
    i32 = jnp.int32
    f32 = jnp.float32
    rows = F * S * NR * L
    dma = pltpu.SemaphoreType.DMA
    filtered = pl.pallas_call(
        step_kernel,
        out_shape=jax.ShapeDtypeStruct((F, S, NR, L, W), f32),
        in_specs=[pl.BlockSpec(memory_space=pltpu.HBM)] * 7,
        out_specs=vmem,
        scratch_shapes=[
            pltpu.SMEM((S,), i32),
            pltpu.SMEM((2, S), i32),
            pltpu.SMEM((NBLK * NR,), i32),
            pltpu.VMEM((F, S, NR, L, W), f32),
            pltpu.VMEM((S, NR, L, W), f32),
            pltpu.VMEM((S, NR, L, W), f32),
            pltpu.VMEM((2, HALF, LANES, 2 * KCUT), jnp.bfloat16),
            pltpu.VMEM((rows, LANES), f32),
            pltpu.VMEM((PIECES, 128), f32),
            pltpu.VMEM((PIECES, 128), f32),
            pltpu.VMEM((2 * PIECES, 128), f32),
            pltpu.VMEM((2 * PIECES, 128), f32),
            pltpu.VMEM((2 * PIECES, 128), f32),
            pltpu.VMEM((2 * PIECES, 128), f32),
            pltpu.VMEM((8, 1280), f32),
            pltpu.VMEM((8, 1280), f32),
            pltpu.VMEM((8, 1280), f32),
            pltpu.VMEM((1280, LANES), f32),
            pltpu.VMEM((1280, LANES), f32),
            pltpu.VMEM((rows, LANES), f32),
            pltpu.VMEM((HALF * ROWS, LANES), f32),
            pltpu.VMEM((HALF * ROWS, LANES), f32),
            pltpu.VMEM((ROWS, 2 * KCUT), f32),
            pltpu.VMEM((ROWS, 2 * KCUT), f32),
            pltpu.VMEM((HALF * ROWS, LANES), f32),
            pltpu.VMEM((HALF * ROWS, LANES), f32),
            dma((6,)), dma, dma, dma, dma, dma,
            dma((2,)), dma((2,)),
            dma((2, HALF)), dma((2, HALF)),
            dma((2,)), dma((2,)),
            dma((2, HALF)), dma((2, HALF)),
        ],
        compiler_params=pltpu.CompilerParams(
            collective_id=0, has_side_effects=True, vmem_limit_bytes=48 << 20),
    )(block_of_slot, face_source.T, cutoff, state, courant_x, courant_y, table)
    return state + filtered


def solution(mesh):
    placed = (
        P(),
        P(None, "lat", None, None, "lon"),
        P("lat", None, None, "lon"),
        P("lat", None, None, "lon"),
        P("lat"),
        P("lat", None),
        P(),
    )
    body = jax.shard_map(
        shards,
        mesh=mesh,
        in_specs=placed,
        out_specs=P(None, "lat", None, None, "lon"),
        check_vma=False,
    )
    table = basis_table()
    return lambda *arrays: body(jnp.asarray(table), *arrays)
```

```python
import math

import jax
import jax.numpy as jnp
import numpy as np
from jax import lax
from jax.experimental import pallas as pl
from jax.experimental.pallas import tpu as pltpu
from jax.sharding import PartitionSpec as P

NLON = 2880
KCUT = 256
F, S, NR, L, W = 5, 3, 8, 8, 180
NBLK, POLAR = 144, 24
LANES = 256
NLAT, NLONDEV, HALF = 48, 16, 8
PIECES = NLAT * 8
INNER, ROWS = 64, 88
MESH = pl.DeviceIdType.MESH


def basis_table():
    column = np.arange(HALF * W, dtype=np.int64)
    phase = ((column[:, None] * np.arange(KCUT)[None, :]) % NLON) * (2.0 * math.pi / NLON)
    table = np.concatenate([np.cos(phase), np.sin(phase)], axis=1).reshape(HALF, W, 2 * KCUT)
    table = np.pad(table, ((0, 0), (0, LANES - W), (0, 0))).astype(np.float32)
    high = table.astype(jnp.bfloat16)
    low = (table - high.astype(np.float32)).astype(jnp.bfloat16)
    return np.stack([high, low])


def split2(x):
    high = x.astype(jnp.bfloat16)
    return high, (x - high.astype(jnp.float32)).astype(jnp.bfloat16)


def split3(x):
    high = x.astype(jnp.bfloat16)
    rest = x - high.astype(jnp.float32)
    mid = rest.astype(jnp.bfloat16)
    return high, mid, (rest - mid.astype(jnp.float32)).astype(jnp.bfloat16)


def dot(a, b, dims):
    return lax.dot_general(a, b, (dims, ((), ())), preferred_element_type=jnp.float32)


def store_rows(main, tail, c, t, value):
    main[pl.ds(c * 64 + t, L, stride=8), :] = value[:, :128]
    tail[pl.ds(c * 64 + t, L, stride=8), :] = value[:, 128:]


def pack(main, tail):
    shape = (NLAT, 8, 128)
    main, tail = main.reshape(shape), tail.reshape(shape)
    sub, lane = iota(shape, 1), iota(shape, 2)
    pairs = jnp.where(lane < 64, tail, pltpu.roll(pltpu.roll(tail, 5, 1), 64, 2))
    first = jnp.where(sub < 6, main, pltpu.roll(pairs, 6, 1))
    return jnp.stack([first, pltpu.roll(pairs, 6, 1)], axis=1).reshape(2 * PIECES, 128)


def unpack(packed):
    shape = (NLAT, 8, 128)
    sub = iota(shape, 1)
    packed = packed.reshape(NLAT, 2, 8, 128)
    first, second = packed[:, 0], packed[:, 1]
    pairs = jnp.where(sub < 2, pltpu.roll(first, 2, 1), pltpu.roll(second, 2, 1))
    tail = jnp.where(sub < 3, pairs, pltpu.roll(pltpu.roll(pairs, 3, 1), 64, 2))
    keep = sub < 6
    main, tail = jnp.where(keep, first, 0.0), jnp.where(keep, tail, 0.0)
    return main.reshape(PIECES, 128), tail.reshape(PIECES, 128)


def pack_asked(main, tail):
    shape = (NLAT, 8, 128)
    main, tail = main.reshape(shape), tail.reshape(shape)
    sub, lane = iota(shape, 1), iota(shape, 2)
    low = lane < 64

    def tails(north, south):
        return jnp.where(low, pltpu.roll(tail, north, 1), pltpu.roll(pltpu.roll(tail, south, 1), 64, 2))

    first = jnp.where(sub < 2, main, jnp.where(sub < 4, pltpu.roll(main, 7, 1), tails(4, 1)))
    second = jnp.where(
        sub < 1, pltpu.roll(main, 6, 1), jnp.where(sub < 2, pltpu.roll(main, 4, 1), tails(0, 5)))
    return jnp.stack([first, second], axis=1).reshape(2 * PIECES, 128)


def load_halo(ref, c, k, south):
    row, tail_row = (k + 2 * south, 4 + k) if k < 2 else (8 + south, 10)
    tail = ref[pl.ds(c * 128 + tail_row, L, stride=16), :]
    if south:
        tail = pltpu.roll(tail, 64, 1)
    return jnp.concatenate([ref[pl.ds(c * 128 + row, L, stride=16), :], tail], axis=1)


def iota(shape, dim):
    return lax.broadcasted_iota(jnp.int32, shape, dim)


def step_kernel(
    block_in, face_in, cut_in, state_in, cx_in, cy_in, table_hbm,
    out_ref,
    block_ref, face_ref, cut_ref, state_ref, cx_ref, cy_ref,
    table, padded, main, tail, send1, got1, send2, halo,
    edges, from_west, from_east,
    tend, rows_out, rows_in, spec, spec_in, smooth_out, smooth_in,
    load_sem, table_sem, s1, r1, s2, r2, s3, r3, edge_send, edge_recv, a_send, a_recv, y_send, y_recv, b_send, b_recv,
):
    lat, lon = lax.axis_index("lat"), lax.axis_index("lon")
    half, seat = lon // HALF, lon % HALF
    partner = (lon + HALF) % NLONDEV
    east, west = (lon + 1) % NLONDEV, (lon + NLONDEV - 1) % NLONDEV

    barrier = pltpu.get_barrier_semaphore()

    @pl.loop(1, NLAT)
    def _(i):
        pl.semaphore_signal(barrier, inc=1, device_id={"lat": (lat + i) % NLAT}, device_id_type=MESH)

    @pl.loop(1, NLONDEV)
    def _(i):
        pl.semaphore_signal(barrier, inc=1, device_id={"lon": (lon + i) % NLONDEV}, device_id_type=MESH)

    loads = [
        pltpu.make_async_copy(source, target, load_sem.at[i])
        for i, (source, target) in enumerate([
            (state_in, state_ref), (cy_in, cy_ref), (face_in, face_ref),
            (block_in, block_ref), (cx_in, cx_ref), (cut_in, cut_ref)])
    ]
    for load in loads:
        load.start()
    main[...] = jnp.zeros_like(main)
    tail[...] = jnp.zeros_like(tail)
    load_table = pltpu.make_async_copy(table_hbm, table, table_sem)
    for load in loads[:4]:
        load.wait()

    cols, keep = [], []
    for t in range(2 * S):
        n = face_ref[t // S, t % S]
        safe = jnp.maximum(n, 0)
        cols.append(jnp.where(n >= 0, 8 * lax.div(safe, S) + lax.rem(safe, S) + (t // S) * S, -1))
        keep.append(jnp.where(n >= 0, 1.0, 0.0))
    keep = keep[S:]
    blocks = [block_ref[s] for s in range(S)]
    polar = [jnp.where(b < POLAR, 1, 0) + jnp.where(b >= NBLK - POLAR, 1, 0) for b in blocks]
    first = (1 - polar[0]) * polar[2]
    picks = [first, 1 + polar[2], 2 - first - polar[2]]
    asks = [
        jnp.where(picks[t % S] == 0, cols[t // S * S], jnp.where(picks[t % S] == 1, cols[t // S * S + 1], cols[t // S * S + 2]))
        for t in range(2 * S)
    ]

    lane = iota((L, LANES), 1)
    zeros = jnp.zeros((L, LANES - W), jnp.float32)

    for t in range(2 * S):
        s = t % S
        want = jnp.full((L, LANES), asks[t].astype(jnp.float32), jnp.float32)
        for f in range(F):
            row = jnp.concatenate([state_ref[f, s, NR - 1 if t < S else 0], zeros], axis=1)
            store_rows(main, tail, f, t, jnp.where(lane == W, want, row))
        if t < S:
            last_wind = jnp.concatenate([cy_ref[s, NR - 1], zeros], axis=1)
            store_rows(main, tail, F, t, jnp.where(lane == W, want, last_wind))
        else:
            store_rows(main, tail, F, t, jnp.where(lane == W, want, 0.0))

    send1[...] = pack(main[...], tail[...])

    pl.semaphore_wait(barrier, NLAT - 1 + NLONDEV - 1)

    def send_pieces(source, target, send_sem, recv_sem, start, size):
        def piece(ref, i):
            return ref.at[pl.ds(pl.multiple_of(i * 16 + start, 8), size), :]

        @pl.loop(1, NLAT)
        def _(i):
            to = (lat + i) % NLAT
            pltpu.make_async_remote_copy(
                piece(source, to), piece(target, lat), send_sem, recv_sem,
                device_id={"lat": to}, device_id_type=MESH).start()

    def wait_pieces(sem, ref, size):
        whole = ref.at[pl.ds(0, size * (NLAT - 1)), :]
        pltpu.make_async_copy(whole, whole, sem).wait()

    mine = pl.ds(pl.multiple_of(lat * 16, 16), 16)
    send_pieces(send1, got1, s1, r1, 0, 9)
    got1[mine, :] = send1[mine, :]

    for load in loads[4:]:
        load.wait()
    narrow = iota((L, 128), 1)

    def lane_of(f, s, r):
        return (f * S + s) * NR + r

    def put_edges(f, ends):
        left, right = ends
        for s in range(S):
            for r in range(NR):
                n = lane_of(f, s, r)
                row = state_ref[f, s, r]
                last = jnp.concatenate([row[:, 128:], zeros], axis=1)
                left = jnp.where(narrow == n, pltpu.roll(row[:, :128], n, 1), left)
                right = jnp.where(narrow == n, pltpu.roll(last, (n + 128 - (W - 1 - 128)) % 128, 1), right)
        return left, right

    nothing = jnp.zeros((L, 128), jnp.float32)
    edges[0], edges[1] = lax.fori_loop(0, F, put_edges, (nothing, nothing))
    right = nothing
    for s in range(S):
        for r in range(NR):
            n = s * NR + r
            last = jnp.concatenate([cx_ref[s, r][:, 128:], zeros], axis=1)
            right = jnp.where(narrow == n, pltpu.roll(last, (n + 128 - (W - 1 - 128)) % 128, 1), right)
    edges[2] = right

    to_west = pltpu.make_async_remote_copy(
        edges, from_east, edge_send.at[0], edge_recv.at[0], device_id={"lon": west}, device_id_type=MESH)
    to_east = pltpu.make_async_remote_copy(
        edges, from_west, edge_send.at[1], edge_recv.at[1], device_id={"lon": east}, device_id_type=MESH)
    to_west.start()
    to_east.start()


    load_table.start()
    padded[...] = jnp.zeros_like(padded)
    padded[:, :W] = state_ref[...].reshape(F * S * NR * L, W)
    rows_out[...] = jnp.zeros_like(rows_out)

    def tile(f, s, r):
        return padded[pl.ds(pl.multiple_of(((f * S + s) * NR + r) * L, L), L), :]

    to_west.wait()
    to_east.wait()

    def tend_row(f, s, r):
        return pl.ds(pl.multiple_of(((s * F + f) * NR + r) * L, L), L)

    def put_tendency(f, s, r, here, merid):
        n = lane_of(f, s, r)
        zonal = jnp.concatenate([cx_ref[s, r], zeros], axis=1)
        beyond = jnp.concatenate([nothing, pltpu.roll(from_east[0], (128 + (W - 1 - 128) - n) % 128, 1)], axis=1)
        to_the_east = jnp.where(lane == W - 1, beyond, pltpu.roll(here, LANES - 1, 1))
        across = zonal * (here + to_the_east) * 0.5
        before = pltpu.roll(from_west[1], (128 - n) % 128, 1)
        cw = pltpu.roll(from_west[2], (128 - s * NR - r) % 128, 1)
        inflow = jnp.concatenate([cw * (before + here[:, :128]) * 0.5, nothing], axis=1)
        from_the_west = jnp.where(lane == 0, inflow, pltpu.roll(across, 1, 1))
        tend[tend_row(f, s, r), :] = jnp.where(lane < W, -((across - from_the_west) + merid), 0.0)

    def wind(s, r):
        return jnp.concatenate([cy_ref[s, r], zeros], axis=1)

    for s in range(S):
        @pl.loop(0, F)
        def _(f):
            here = tile(f, s, 1)
            flux = wind(s, 0) * (tile(f, s, 0) + here) * 0.5
            for r in range(1, NR - 1):
                after = tile(f, s, r + 1)
                next_flux = wind(s, r) * (here + after) * 0.5
                put_tendency(f, s, r, here, next_flux - flux)
                flux, here = next_flux, after

    def spot(r, k, f):
        if 0 < r < NR - 1:
            n = ((r - 1) * 2 + k) * F + f
            return (n // 8) * ROWS + (n % 8) * L
        n = ((r // (NR - 1)) * 2 + k) * F + f
        return (n // 3) * ROWS + INNER + (n % 3) * L

    def spot_rows(r, k, f):
        return pl.ds(pl.multiple_of(spot(r, k, f), L), L)

    uppers = [jnp.full((L, LANES), picks[k], jnp.int32) == k + 1 for k in range(2)]

    def gather_rows(rs):
        for k in range(2):
            @pl.loop(0, F)
            def _(f):
                for r in rs:
                    low, high = tend[tend_row(f, k, r), :], tend[tend_row(f, k + 1, r), :]
                    rows_out[spot_rows(r, k, f), :] = jnp.where(uppers[k], high, low)

    starts, sizes = (0, INNER), (INNER, ROWS - INNER)

    def part(g, i):
        return pl.ds(pl.multiple_of(i * ROWS + starts[g], L), sizes[g])

    def seat_copy(g, i, source, target, send_sem, recv_sem):
        to = (seat + i) % HALF
        return pltpu.make_async_remote_copy(
            source.at[part(g, to), :], target.at[part(g, seat), :], send_sem.at[g, to], recv_sem.at[g, seat],
            device_id={"lon": half * HALF + to}, device_id_type=MESH)

    def seat_wait(g, i, source, target, send_sem, recv_sem):
        other = (seat + HALF - i) % HALF
        pltpu.make_async_remote_copy(
            source.at[part(g, other), :], target.at[part(g, other), :], send_sem.at[g, other],
            recv_sem.at[g, other], device_id={"lon": half * HALF + other}, device_id_type=MESH).wait_recv()

    there = (rows_out, rows_in, a_send, a_recv)
    back = (smooth_out, smooth_in, b_send, b_recv)

    def exchange(g, way):
        for i in range(1, HALF):
            seat_copy(g, i, *way).start()
        way[1][part(g, seat), :] = way[0][part(g, seat), :]

    def arrive(g, way):
        for i in range(1, HALF):
            seat_wait(g, i, *way)

    def leave(g, way):
        for i in range(1, HALF):
            seat_copy(g, i, *way).wait_send()

    nn, nt = ((1,), (0,)), ((1,), (1,))

    def product(xh, xl, d, dims):
        rows = xh.shape[0]
        both = dot(jnp.concatenate([xh, xl], axis=0), table[0, d], dims)
        return both[:rows] + (both[rows:] + dot(xh, table[1, d], dims))

    def forward(g):
        total = jnp.zeros((sizes[g], 2 * KCUT), jnp.float32)
        for d in range(HALF):
            xh, xl = split2(rows_in[d * ROWS + starts[g]:d * ROWS + starts[g] + sizes[g], :])
            total += product(xh, xl, d, nn)
        spec[starts[g]:starts[g] + sizes[g], :] = total

    def swap(g):
        rows = pl.ds(starts[g], sizes[g])
        return pltpu.make_async_remote_copy(
            spec.at[rows, :], spec_in.at[rows, :], y_send.at[g], y_recv.at[g],
            device_id={"lon": partner}, device_id_type=MESH)

    chosen = [jnp.where(picks[k] == k + 1, blocks[k + 1], blocks[k]) for k in range(2)]

    def limits(g):
        parts = []
        for j in range(sizes[g] // L):
            if g == 0:
                n = seat * 8 + j
                r = 1 + n // (2 * F)
            else:
                n = seat * 3 + j
                r = jnp.minimum(n // (2 * F), 1) * (NR - 1)
            block = jnp.where((n // F) % 2 == 0, chosen[0], chosen[1])
            parts.append(jnp.full((L, 2 * KCUT), cut_ref[block * NR + r], jnp.int32))
        return jnp.concatenate(parts, axis=0)

    def inverse(g):
        shape = (sizes[g], 2 * KCUT)
        wave = iota(shape, 1) % KCUT
        sign = jnp.where(wave % 2 == 0, 1.0, -1.0)
        scale = jnp.where(wave == 0, 1.0 / NLON, 2.0 / NLON)
        rows = slice(starts[g], starts[g] + sizes[g])
        weights = jnp.where(wave < limits(g), scale, 0.0)
        xh, xl = split2((spec[rows, :] + sign * spec_in[rows, :]) * weights)
        for d in range(HALF):
            smooth_out[d * ROWS + starts[g]:d * ROWS + starts[g] + sizes[g], :] = product(xh, xl, d, nt)

    gather_rows(range(1, NR - 1))
    exchange(0, there)

    wait_pieces(r1, got1, 9)
    pieces = jnp.concatenate(unpack(got1[...]), axis=1)
    asked = jnp.broadcast_to(pieces[:, W:W + 1], (PIECES, PIECES))
    onehot = jnp.where(asked == iota((PIECES, PIECES), 1).astype(jnp.float32), 1.0, 0.0).astype(jnp.bfloat16)
    a, b, c = split3(pieces)
    found = (dot(onehot, a, nn) + dot(onehot, b, nn)) + dot(onehot, c, nn)
    send2[...] = pack_asked(found[:, :128], found[:, 128:])
    send_pieces(send2, halo, s2, r2, 0, 6)
    send_pieces(send2, halo, s3, r3, 8, 3)
    halo[mine, :] = send2[mine, :]

    load_table.wait()
    arrive(0, there)
    forward(0)
    swap(0).start()

    at_pick = [[jnp.full((L, LANES), picks[k], jnp.int32) == s for k in range(S)] for s in range(S)]

    def outer_rows(known):
        for s in range(S):
            kept = jnp.full((L, LANES), keep[s], jnp.float32)

            def halo_row(c, south):
                row = load_halo(halo, c, 1, south)
                for k in known:
                    row = jnp.where(at_pick[s][k], load_halo(halo, c, k, south), row)
                return row

            @pl.loop(0, F)
            def _(f):
                above, below, north_wind = halo_row(f, 0), halo_row(f, 1), halo_row(F, 0)
                here, after = tile(f, s, 0), tile(f, s, 1)
                put_tendency(
                    f, s, 0, here, wind(s, 0) * (here + after) * 0.5 - north_wind * (above + here) * 0.5)
                before, here = tile(f, s, NR - 2), tile(f, s, NR - 1)
                put_tendency(
                    f, s, NR - 1, here,
                    wind(s, NR - 1) * (here + below) * 0.5 * kept - wind(s, NR - 2) * (before + here) * 0.5)

    wait_pieces(r2, halo, 6)
    outer_rows((0,))
    gather_rows((0, NR - 1))
    exchange(1, there)

    swap(0).wait()
    inverse(0)
    exchange(0, back)

    arrive(1, there)
    forward(1)
    swap(1).start()
    wait_pieces(r3, halo, 3)
    outer_rows((0, 2))
    swap(1).wait()
    inverse(1)
    exchange(1, back)

    uses = [
        [jnp.full((L, LANES), jnp.where(picks[k] == s, polar[s], 0), jnp.int32) > 0 for k in range(2)]
        for s in range(S)
    ]

    def finish(rs):
        for s in range(S):
            @pl.loop(0, F)
            def _(f):
                for r in rs:
                    value = tend[tend_row(f, s, r), :]
                    for k in range(2):
                        value = jnp.where(uses[s][k], smooth_in[spot_rows(r, k, f), :], value)
                    out_ref[f, s, r] = value[:, :W]

    arrive(0, back)
    finish(range(1, NR - 1))
    arrive(1, back)
    finish((0, NR - 1))

    wait_pieces(s1, send1, 9)
    wait_pieces(s2, send2, 6)
    wait_pieces(s3, send2, 3)
    for g in range(2):
        leave(g, there)
        leave(g, back)


def shards(table, state, courant_x, courant_y, block_of_slot, face_source, cutoff):
    vmem = pl.BlockSpec(memory_space=pltpu.VMEM)
    i32 = jnp.int32
    f32 = jnp.float32
    rows = F * S * NR * L
    dma = pltpu.SemaphoreType.DMA
    filtered = pl.pallas_call(
        step_kernel,
        out_shape=jax.ShapeDtypeStruct((F, S, NR, L, W), f32),
        in_specs=[pl.BlockSpec(memory_space=pltpu.HBM)] * 7,
        out_specs=vmem,
        scratch_shapes=[
            pltpu.SMEM((S,), i32),
            pltpu.SMEM((2, S), i32),
            pltpu.SMEM((NBLK * NR,), i32),
            pltpu.VMEM((F, S, NR, L, W), f32),
            pltpu.VMEM((S, NR, L, W), f32),
            pltpu.VMEM((S, NR, L, W), f32),
            pltpu.VMEM((2, HALF, LANES, 2 * KCUT), jnp.bfloat16),
            pltpu.VMEM((rows, LANES), f32),
            pltpu.VMEM((PIECES, 128), f32),
            pltpu.VMEM((PIECES, 128), f32),
            pltpu.VMEM((2 * PIECES, 128), f32),
            pltpu.VMEM((2 * PIECES, 128), f32),
            pltpu.VMEM((2 * PIECES, 128), f32),
            pltpu.VMEM((2 * PIECES, 128), f32),
            pltpu.VMEM((3, L, 128), f32),
            pltpu.VMEM((3, L, 128), f32),
            pltpu.VMEM((3, L, 128), f32),
            pltpu.VMEM((rows, LANES), f32),
            pltpu.VMEM((HALF * ROWS, LANES), f32),
            pltpu.VMEM((HALF * ROWS, LANES), f32),
            pltpu.VMEM((ROWS, 2 * KCUT), f32),
            pltpu.VMEM((ROWS, 2 * KCUT), f32),
            pltpu.VMEM((HALF * ROWS, LANES), f32),
            pltpu.VMEM((HALF * ROWS, LANES), f32),
            dma((6,)), dma, dma, dma, dma, dma, dma, dma,
            dma((2,)), dma((2,)),
            dma((2, HALF)), dma((2, HALF)),
            dma((2,)), dma((2,)),
            dma((2, HALF)), dma((2, HALF)),
        ],
        compiler_params=pltpu.CompilerParams(
            collective_id=0, has_side_effects=True, vmem_limit_bytes=48 << 20),
    )(block_of_slot, face_source.T, cutoff, state, courant_x, courant_y, table)
    return state + filtered


def solution(mesh):
    placed = (
        P(),
        P(None, "lat", None, None, "lon"),
        P("lat", None, None, "lon"),
        P("lat", None, None, "lon"),
        P("lat"),
        P("lat", None),
        P(),
    )
    body = jax.shard_map(
        shards,
        mesh=mesh,
        in_specs=placed,
        out_specs=P(None, "lat", None, None, "lon"),
        check_vma=False,
    )
    table = basis_table()
    return lambda *arrays: body(jnp.asarray(table), *arrays)
```

```python
import math

import jax
import jax.numpy as jnp
import numpy as np
from jax import lax
from jax.experimental import pallas as pl
from jax.experimental.pallas import tpu as pltpu
from jax.sharding import PartitionSpec as P

NLON = 2880
KCUT = 256
F, S, NR, L, W = 5, 3, 8, 8, 180
NBLK, POLAR = 144, 24
LANES = 256
NLAT, NLONDEV, HALF = 48, 16, 8
PIECES = NLAT * 8
INNER, ROWS = 64, 88
MESH = pl.DeviceIdType.MESH


def basis_table():
    column = np.arange(HALF * W, dtype=np.int64)
    phase = ((column[:, None] * np.arange(KCUT)[None, :]) % NLON) * (2.0 * math.pi / NLON)
    table = np.concatenate([np.cos(phase), np.sin(phase)], axis=1).reshape(HALF, W, 2 * KCUT)
    table = np.pad(table, ((0, 0), (0, LANES - W), (0, 0))).astype(np.float32)
    high = table.astype(jnp.bfloat16)
    low = (table - high.astype(np.float32)).astype(jnp.bfloat16)
    return np.stack([high, low])


def split2(x):
    high = x.astype(jnp.bfloat16)
    return high, (x - high.astype(jnp.float32)).astype(jnp.bfloat16)


def split3(x):
    high = x.astype(jnp.bfloat16)
    rest = x - high.astype(jnp.float32)
    mid = rest.astype(jnp.bfloat16)
    return high, mid, (rest - mid.astype(jnp.float32)).astype(jnp.bfloat16)


def dot(a, b, dims):
    return lax.dot_general(a, b, (dims, ((), ())), preferred_element_type=jnp.float32)


def store_rows(main, tail, c, t, value):
    main[pl.ds(c * 64 + t, L, stride=8), :] = value[:, :128]
    tail[pl.ds(c * 64 + t, L, stride=8), :] = value[:, 128:]


def pack(main, tail):
    shape = (NLAT, 8, 128)
    main, tail = main.reshape(shape), tail.reshape(shape)
    sub, lane = iota(shape, 1), iota(shape, 2)
    pairs = jnp.where(lane < 64, tail, pltpu.roll(pltpu.roll(tail, 5, 1), 64, 2))
    first = jnp.where(sub < 6, main, pltpu.roll(pairs, 6, 1))
    return jnp.stack([first, pltpu.roll(pairs, 6, 1)], axis=1).reshape(2 * PIECES, 128)


def unpack(packed):
    shape = (NLAT, 8, 128)
    sub = iota(shape, 1)
    packed = packed.reshape(NLAT, 2, 8, 128)
    first, second = packed[:, 0], packed[:, 1]
    pairs = jnp.where(sub < 2, pltpu.roll(first, 2, 1), pltpu.roll(second, 2, 1))
    tail = jnp.where(sub < 3, pairs, pltpu.roll(pltpu.roll(pairs, 3, 1), 64, 2))
    keep = sub < 6
    main, tail = jnp.where(keep, first, 0.0), jnp.where(keep, tail, 0.0)
    return main.reshape(PIECES, 128), tail.reshape(PIECES, 128)


def pack_asked(main, tail):
    shape = (NLAT, 8, 128)
    main, tail = main.reshape(shape), tail.reshape(shape)
    sub, lane = iota(shape, 1), iota(shape, 2)
    low = lane < 64

    def tails(north, south):
        return jnp.where(low, pltpu.roll(tail, north, 1), pltpu.roll(pltpu.roll(tail, south, 1), 64, 2))

    first = jnp.where(sub < 2, main, jnp.where(sub < 4, pltpu.roll(main, 7, 1), tails(4, 1)))
    second = jnp.where(
        sub < 1, pltpu.roll(main, 6, 1), jnp.where(sub < 2, pltpu.roll(main, 4, 1), tails(0, 5)))
    return jnp.stack([first, second], axis=1).reshape(2 * PIECES, 128)


def load_halo(ref, c, k, south):
    row, tail_row = (k + 2 * south, 4 + k) if k < 2 else (8 + south, 10)
    tail = ref[pl.ds(c * 128 + tail_row, L, stride=16), :]
    if south:
        tail = pltpu.roll(tail, 64, 1)
    return jnp.concatenate([ref[pl.ds(c * 128 + row, L, stride=16), :], tail], axis=1)


def iota(shape, dim):
    return lax.broadcasted_iota(jnp.int32, shape, dim)


def step_kernel(
    block_in, face_in, cut_in, state_in, cx_in, cy_in, table_hbm,
    out_ref,
    block_ref, face_ref, cut_ref, state_ref, cx_ref, cy_ref,
    table, padded, main, tail, send1, got1, send2, halo,
    edges, from_west, from_east,
    tend, rows_out, rows_in, spec, spec_in, smooth_out, smooth_in,
    load_sem, table_sem, s1, r1, s2, r2, s3, r3, edge_send, edge_recv, a_send, a_recv, y_send, y_recv, b_send, b_recv,
):
    lat, lon = lax.axis_index("lat"), lax.axis_index("lon")
    half, seat = lon // HALF, lon % HALF
    partner = (lon + HALF) % NLONDEV
    east, west = (lon + 1) % NLONDEV, (lon + NLONDEV - 1) % NLONDEV

    barrier = pltpu.get_barrier_semaphore()

    @pl.loop(1, NLAT)
    def _(i):
        pl.semaphore_signal(barrier, inc=1, device_id={"lat": (lat + i) % NLAT}, device_id_type=MESH)

    @pl.loop(1, NLONDEV)
    def _(i):
        pl.semaphore_signal(barrier, inc=1, device_id={"lon": (lon + i) % NLONDEV}, device_id_type=MESH)

    loads = [
        pltpu.make_async_copy(source, target, load_sem.at[i])
        for i, (source, target) in enumerate([
            (state_in, state_ref), (cy_in, cy_ref), (face_in, face_ref),
            (block_in, block_ref), (cx_in, cx_ref), (cut_in, cut_ref)])
    ]
    for load in loads:
        load.start()
    main[...] = jnp.zeros_like(main)
    tail[...] = jnp.zeros_like(tail)
    load_table = pltpu.make_async_copy(table_hbm, table, table_sem)
    for load in loads[:4]:
        load.wait()

    cols, keep = [], []
    for t in range(2 * S):
        n = face_ref[t // S, t % S]
        safe = jnp.maximum(n, 0)
        cols.append(jnp.where(n >= 0, 8 * lax.div(safe, S) + lax.rem(safe, S) + (t // S) * S, -1))
        keep.append(jnp.where(n >= 0, 1.0, 0.0))
    keep = keep[S:]
    blocks = [block_ref[s] for s in range(S)]
    polar = [jnp.where(b < POLAR, 1, 0) + jnp.where(b >= NBLK - POLAR, 1, 0) for b in blocks]
    first = (1 - polar[0]) * polar[2]
    picks = [first, 1 + polar[2], 2 - first - polar[2]]
    asks = [
        jnp.where(picks[t % S] == 0, cols[t // S * S], jnp.where(picks[t % S] == 1, cols[t // S * S + 1], cols[t // S * S + 2]))
        for t in range(2 * S)
    ]

    lane = iota((L, LANES), 1)
    zeros = jnp.zeros((L, LANES - W), jnp.float32)

    for t in range(2 * S):
        s = t % S
        want = jnp.full((L, LANES), asks[t].astype(jnp.float32), jnp.float32)
        for f in range(F):
            row = jnp.concatenate([state_ref[f, s, NR - 1 if t < S else 0], zeros], axis=1)
            store_rows(main, tail, f, t, jnp.where(lane == W, want, row))
        if t < S:
            last_wind = jnp.concatenate([cy_ref[s, NR - 1], zeros], axis=1)
            store_rows(main, tail, F, t, jnp.where(lane == W, want, last_wind))
        else:
            store_rows(main, tail, F, t, jnp.where(lane == W, want, 0.0))

    send1[...] = pack(main[...], tail[...])

    pl.semaphore_wait(barrier, NLAT - 1 + NLONDEV - 1)

    def send_pieces(source, target, send_sem, recv_sem, start, size):
        def piece(ref, i):
            return ref.at[pl.ds(pl.multiple_of(i * 16 + start, 8), size), :]

        @pl.loop(0, NLAT - 1)
        def _(i):
            turn = i // 4
            along = 6 + (1 - 2 * (turn % 2)) * ((turn + 1) // 2)
            to = ((lat // 12 + 3 - i % 4) % 4) * 12 + (lat % 12 + along) % 12
            pltpu.make_async_remote_copy(
                piece(source, to), piece(target, lat), send_sem, recv_sem,
                device_id={"lat": to}, device_id_type=MESH).start()

    def wait_pieces(sem, ref, size):
        whole = ref.at[pl.ds(0, size * (NLAT - 1)), :]
        pltpu.make_async_copy(whole, whole, sem).wait()

    mine = pl.ds(pl.multiple_of(lat * 16, 16), 16)
    send_pieces(send1, got1, s1, r1, 0, 9)
    got1[mine, :] = send1[mine, :]

    for load in loads[4:]:
        load.wait()
    narrow = iota((L, 128), 1)

    def lane_of(f, s, r):
        return (f * S + s) * NR + r

    def put_edges(f, ends):
        left, right = ends
        for s in range(S):
            for r in range(NR):
                n = lane_of(f, s, r)
                row = state_ref[f, s, r]
                last = jnp.concatenate([row[:, 128:], zeros], axis=1)
                left = jnp.where(narrow == n, pltpu.roll(row[:, :128], n, 1), left)
                right = jnp.where(narrow == n, pltpu.roll(last, (n + 128 - (W - 1 - 128)) % 128, 1), right)
        return left, right

    nothing = jnp.zeros((L, 128), jnp.float32)
    edges[0], edges[1] = lax.fori_loop(0, F, put_edges, (nothing, nothing))
    right = nothing
    for s in range(S):
        for r in range(NR):
            n = s * NR + r
            last = jnp.concatenate([cx_ref[s, r][:, 128:], zeros], axis=1)
            right = jnp.where(narrow == n, pltpu.roll(last, (n + 128 - (W - 1 - 128)) % 128, 1), right)
    edges[2] = right

    to_west = pltpu.make_async_remote_copy(
        edges, from_east, edge_send.at[0], edge_recv.at[0], device_id={"lon": west}, device_id_type=MESH)
    to_east = pltpu.make_async_remote_copy(
        edges, from_west, edge_send.at[1], edge_recv.at[1], device_id={"lon": east}, device_id_type=MESH)
    to_west.start()
    to_east.start()


    load_table.start()
    padded[...] = jnp.zeros_like(padded)
    padded[:, :W] = state_ref[...].reshape(F * S * NR * L, W)
    rows_out[...] = jnp.zeros_like(rows_out)

    def tile(f, s, r):
        return padded[pl.ds(pl.multiple_of(((f * S + s) * NR + r) * L, L), L), :]

    to_west.wait()
    to_east.wait()

    def tend_row(f, s, r):
        return pl.ds(pl.multiple_of(((s * F + f) * NR + r) * L, L), L)

    def put_tendency(f, s, r, here, merid):
        n = lane_of(f, s, r)
        zonal = jnp.concatenate([cx_ref[s, r], zeros], axis=1)
        beyond = jnp.concatenate([nothing, pltpu.roll(from_east[0], (128 + (W - 1 - 128) - n) % 128, 1)], axis=1)
        to_the_east = jnp.where(lane == W - 1, beyond, pltpu.roll(here, LANES - 1, 1))
        across = zonal * (here + to_the_east) * 0.5
        before = pltpu.roll(from_west[1], (128 - n) % 128, 1)
        cw = pltpu.roll(from_west[2], (128 - s * NR - r) % 128, 1)
        inflow = jnp.concatenate([cw * (before + here[:, :128]) * 0.5, nothing], axis=1)
        from_the_west = jnp.where(lane == 0, inflow, pltpu.roll(across, 1, 1))
        tend[tend_row(f, s, r), :] = jnp.where(lane < W, -((across - from_the_west) + merid), 0.0)

    def wind(s, r):
        return jnp.concatenate([cy_ref[s, r], zeros], axis=1)

    for s in range(S):
        @pl.loop(0, F)
        def _(f):
            here = tile(f, s, 1)
            flux = wind(s, 0) * (tile(f, s, 0) + here) * 0.5
            for r in range(1, NR - 1):
                after = tile(f, s, r + 1)
                next_flux = wind(s, r) * (here + after) * 0.5
                put_tendency(f, s, r, here, next_flux - flux)
                flux, here = next_flux, after

    def spot(r, k, f):
        if 0 < r < NR - 1:
            n = ((r - 1) * 2 + k) * F + f
            return (n // 8) * ROWS + (n % 8) * L
        n = ((r // (NR - 1)) * 2 + k) * F + f
        return (n // 3) * ROWS + INNER + (n % 3) * L

    def spot_rows(r, k, f):
        return pl.ds(pl.multiple_of(spot(r, k, f), L), L)

    uppers = [jnp.full((L, LANES), picks[k], jnp.int32) == k + 1 for k in range(2)]

    def gather_rows(rs):
        for k in range(2):
            @pl.loop(0, F)
            def _(f):
                for r in rs:
                    low, high = tend[tend_row(f, k, r), :], tend[tend_row(f, k + 1, r), :]
                    rows_out[spot_rows(r, k, f), :] = jnp.where(uppers[k], high, low)

    starts, sizes = (0, INNER), (INNER, ROWS - INNER)

    def part(g, i):
        return pl.ds(pl.multiple_of(i * ROWS + starts[g], L), sizes[g])

    def seat_copy(g, i, source, target, send_sem, recv_sem):
        to = (seat + i) % HALF
        return pltpu.make_async_remote_copy(
            source.at[part(g, to), :], target.at[part(g, seat), :], send_sem.at[g, to], recv_sem.at[g, seat],
            device_id={"lon": half * HALF + to}, device_id_type=MESH)

    def seat_wait(g, i, source, target, send_sem, recv_sem):
        other = (seat + HALF - i) % HALF
        pltpu.make_async_remote_copy(
            source.at[part(g, other), :], target.at[part(g, other), :], send_sem.at[g, other],
            recv_sem.at[g, other], device_id={"lon": half * HALF + other}, device_id_type=MESH).wait_recv()

    there = (rows_out, rows_in, a_send, a_recv)
    back = (smooth_out, smooth_in, b_send, b_recv)

    def exchange(g, way):
        for i in range(1, HALF):
            seat_copy(g, i, *way).start()
        way[1][part(g, seat), :] = way[0][part(g, seat), :]

    def arrive(g, way):
        for i in range(1, HALF):
            seat_wait(g, i, *way)

    def leave(g, way):
        for i in range(1, HALF):
            seat_copy(g, i, *way).wait_send()

    nn, nt = ((1,), (0,)), ((1,), (1,))

    def product(xh, xl, d, dims):
        rows = xh.shape[0]
        both = dot(jnp.concatenate([xh, xl], axis=0), table[0, d], dims)
        return both[:rows] + (both[rows:] + dot(xh, table[1, d], dims))

    def forward(g):
        total = jnp.zeros((sizes[g], 2 * KCUT), jnp.float32)
        for d in range(HALF):
            xh, xl = split2(rows_in[d * ROWS + starts[g]:d * ROWS + starts[g] + sizes[g], :])
            total += product(xh, xl, d, nn)
        spec[starts[g]:starts[g] + sizes[g], :] = total

    def swap(g):
        rows = pl.ds(starts[g], sizes[g])
        return pltpu.make_async_remote_copy(
            spec.at[rows, :], spec_in.at[rows, :], y_send.at[g], y_recv.at[g],
            device_id={"lon": partner}, device_id_type=MESH)

    chosen = [jnp.where(picks[k] == k + 1, blocks[k + 1], blocks[k]) for k in range(2)]

    def limits(g):
        parts = []
        for j in range(sizes[g] // L):
            if g == 0:
                n = seat * 8 + j
                r = 1 + n // (2 * F)
            else:
                n = seat * 3 + j
                r = jnp.minimum(n // (2 * F), 1) * (NR - 1)
            block = jnp.where((n // F) % 2 == 0, chosen[0], chosen[1])
            parts.append(jnp.full((L, 2 * KCUT), cut_ref[block * NR + r], jnp.int32))
        return jnp.concatenate(parts, axis=0)

    def inverse(g):
        shape = (sizes[g], 2 * KCUT)
        wave = iota(shape, 1) % KCUT
        sign = jnp.where(wave % 2 == 0, 1.0, -1.0)
        scale = jnp.where(wave == 0, 1.0 / NLON, 2.0 / NLON)
        rows = slice(starts[g], starts[g] + sizes[g])
        weights = jnp.where(wave < limits(g), scale, 0.0)
        xh, xl = split2((spec[rows, :] + sign * spec_in[rows, :]) * weights)
        for d in range(HALF):
            smooth_out[d * ROWS + starts[g]:d * ROWS + starts[g] + sizes[g], :] = product(xh, xl, d, nt)

    gather_rows(range(1, NR - 1))
    exchange(0, there)

    wait_pieces(r1, got1, 9)
    pieces = jnp.concatenate(unpack(got1[...]), axis=1)
    asked = jnp.broadcast_to(pieces[:, W:W + 1], (PIECES, PIECES))
    onehot = jnp.where(asked == iota((PIECES, PIECES), 1).astype(jnp.float32), 1.0, 0.0).astype(jnp.bfloat16)
    a, b, c = split3(pieces)
    found = (dot(onehot, a, nn) + dot(onehot, b, nn)) + dot(onehot, c, nn)
    send2[...] = pack_asked(found[:, :128], found[:, 128:])
    send_pieces(send2, halo, s2, r2, 0, 6)
    halo[mine, :] = send2[mine, :]

    load_table.wait()
    arrive(0, there)
    forward(0)
    swap(0).start()
    send_pieces(send2, halo, s3, r3, 8, 3)

    at_pick = [[jnp.full((L, LANES), picks[k], jnp.int32) == s for k in range(S)] for s in range(S)]

    def outer_rows(known):
        for s in range(S):
            kept = jnp.full((L, LANES), keep[s], jnp.float32)

            def halo_row(c, south):
                row = load_halo(halo, c, 1, south)
                for k in known:
                    row = jnp.where(at_pick[s][k], load_halo(halo, c, k, south), row)
                return row

            @pl.loop(0, F)
            def _(f):
                above, below, north_wind = halo_row(f, 0), halo_row(f, 1), halo_row(F, 0)
                here, after = tile(f, s, 0), tile(f, s, 1)
                put_tendency(
                    f, s, 0, here, wind(s, 0) * (here + after) * 0.5 - north_wind * (above + here) * 0.5)
                before, here = tile(f, s, NR - 2), tile(f, s, NR - 1)
                put_tendency(
                    f, s, NR - 1, here,
                    wind(s, NR - 1) * (here + below) * 0.5 * kept - wind(s, NR - 2) * (before + here) * 0.5)

    wait_pieces(r2, halo, 6)
    outer_rows((0,))
    gather_rows((0, NR - 1))
    exchange(1, there)

    swap(0).wait()
    inverse(0)
    exchange(0, back)

    arrive(1, there)
    forward(1)
    swap(1).start()
    wait_pieces(r3, halo, 3)
    outer_rows((0, 2))
    swap(1).wait()
    inverse(1)
    exchange(1, back)

    uses = [
        [jnp.full((L, LANES), jnp.where(picks[k] == s, polar[s], 0), jnp.int32) > 0 for k in range(2)]
        for s in range(S)
    ]

    def finish(rs):
        for s in range(S):
            @pl.loop(0, F)
            def _(f):
                for r in rs:
                    value = tend[tend_row(f, s, r), :]
                    for k in range(2):
                        value = jnp.where(uses[s][k], smooth_in[spot_rows(r, k, f), :], value)
                    out_ref[f, s, r] = value[:, :W]

    arrive(0, back)
    finish(range(1, NR - 1))
    arrive(1, back)
    finish((0, NR - 1))

    wait_pieces(s1, send1, 9)
    wait_pieces(s2, send2, 6)
    wait_pieces(s3, send2, 3)
    for g in range(2):
        leave(g, there)
        leave(g, back)


def shards(table, state, courant_x, courant_y, block_of_slot, face_source, cutoff):
    vmem = pl.BlockSpec(memory_space=pltpu.VMEM)
    i32 = jnp.int32
    f32 = jnp.float32
    rows = F * S * NR * L
    dma = pltpu.SemaphoreType.DMA
    filtered = pl.pallas_call(
        step_kernel,
        out_shape=jax.ShapeDtypeStruct((F, S, NR, L, W), f32),
        in_specs=[pl.BlockSpec(memory_space=pltpu.HBM)] * 7,
        out_specs=vmem,
        scratch_shapes=[
            pltpu.SMEM((S,), i32),
            pltpu.SMEM((2, S), i32),
            pltpu.SMEM((NBLK * NR,), i32),
            pltpu.VMEM((F, S, NR, L, W), f32),
            pltpu.VMEM((S, NR, L, W), f32),
            pltpu.VMEM((S, NR, L, W), f32),
            pltpu.VMEM((2, HALF, LANES, 2 * KCUT), jnp.bfloat16),
            pltpu.VMEM((rows, LANES), f32),
            pltpu.VMEM((PIECES, 128), f32),
            pltpu.VMEM((PIECES, 128), f32),
            pltpu.VMEM((2 * PIECES, 128), f32),
            pltpu.VMEM((2 * PIECES, 128), f32),
            pltpu.VMEM((2 * PIECES, 128), f32),
            pltpu.VMEM((2 * PIECES, 128), f32),
            pltpu.VMEM((3, L, 128), f32),
            pltpu.VMEM((3, L, 128), f32),
            pltpu.VMEM((3, L, 128), f32),
            pltpu.VMEM((rows, LANES), f32),
            pltpu.VMEM((HALF * ROWS, LANES), f32),
            pltpu.VMEM((HALF * ROWS, LANES), f32),
            pltpu.VMEM((ROWS, 2 * KCUT), f32),
            pltpu.VMEM((ROWS, 2 * KCUT), f32),
            pltpu.VMEM((HALF * ROWS, LANES), f32),
            pltpu.VMEM((HALF * ROWS, LANES), f32),
            dma((6,)), dma, dma, dma, dma, dma, dma, dma,
            dma((2,)), dma((2,)),
            dma((2, HALF)), dma((2, HALF)),
            dma((2,)), dma((2,)),
            dma((2, HALF)), dma((2, HALF)),
        ],
        compiler_params=pltpu.CompilerParams(
            collective_id=0, has_side_effects=True, vmem_limit_bytes=48 << 20),
    )(block_of_slot, face_source.T, cutoff, state, courant_x, courant_y, table)
    return state + filtered


def solution(mesh):
    placed = (
        P(),
        P(None, "lat", None, None, "lon"),
        P("lat", None, None, "lon"),
        P("lat", None, None, "lon"),
        P("lat"),
        P("lat", None),
        P(),
    )
    body = jax.shard_map(
        shards,
        mesh=mesh,
        in_specs=placed,
        out_specs=P(None, "lat", None, None, "lon"),
        check_vma=False,
    )
    table = basis_table()
    return lambda *arrays: body(jnp.asarray(table), *arrays)
```

```python
import math

import jax
import jax.numpy as jnp
import numpy as np
from jax import lax
from jax.experimental import pallas as pl
from jax.experimental.pallas import tpu as pltpu
from jax.sharding import PartitionSpec as P

NLON = 2880
KCUT = 256
F, S, NR, L, W = 5, 3, 8, 8, 180
NBLK, POLAR = 144, 24
LANES = 256
NLAT, NLONDEV, HALF = 48, 16, 8
PIECES = NLAT * 8
INNER, ROWS = 64, 88
MESH = pl.DeviceIdType.MESH


def basis_table():
    column = np.arange(HALF * W, dtype=np.int64)
    phase = ((column[:, None] * np.arange(KCUT)[None, :]) % NLON) * (2.0 * math.pi / NLON)
    table = np.concatenate([np.cos(phase), np.sin(phase)], axis=1).reshape(HALF, W, 2 * KCUT)
    table = np.pad(table, ((0, 0), (0, LANES - W), (0, 0))).astype(np.float32)
    high = table.astype(jnp.bfloat16)
    low = (table - high.astype(np.float32)).astype(jnp.bfloat16)
    return np.stack([high, low])


def split2(x):
    high = x.astype(jnp.bfloat16)
    return high, (x - high.astype(jnp.float32)).astype(jnp.bfloat16)


def split3(x):
    high = x.astype(jnp.bfloat16)
    rest = x - high.astype(jnp.float32)
    mid = rest.astype(jnp.bfloat16)
    return high, mid, (rest - mid.astype(jnp.float32)).astype(jnp.bfloat16)


def dot(a, b, dims):
    return lax.dot_general(a, b, (dims, ((), ())), preferred_element_type=jnp.float32)


def store_rows(main, tail, c, t, value):
    main[pl.ds(c * 64 + t, L, stride=8), :] = value[:, :128]
    tail[pl.ds(c * 64 + t, L, stride=8), :] = value[:, 128:]


def pack(main, tail):
    shape = (NLAT, 8, 128)
    main, tail = main.reshape(shape), tail.reshape(shape)
    sub, lane = iota(shape, 1), iota(shape, 2)
    pairs = jnp.where(lane < 64, tail, pltpu.roll(pltpu.roll(tail, 5, 1), 64, 2))
    first = jnp.where(sub < 6, main, pltpu.roll(pairs, 6, 1))
    return jnp.stack([first, pltpu.roll(pairs, 6, 1)], axis=1).reshape(2 * PIECES, 128)


def unpack(packed):
    shape = (NLAT, 8, 128)
    sub = iota(shape, 1)
    packed = packed.reshape(NLAT, 2, 8, 128)
    first, second = packed[:, 0], packed[:, 1]
    pairs = jnp.where(sub < 2, pltpu.roll(first, 2, 1), pltpu.roll(second, 2, 1))
    tail = jnp.where(sub < 3, pairs, pltpu.roll(pltpu.roll(pairs, 3, 1), 64, 2))
    keep = sub < 6
    main, tail = jnp.where(keep, first, 0.0), jnp.where(keep, tail, 0.0)
    return main.reshape(PIECES, 128), tail.reshape(PIECES, 128)


def pack_asked(main, tail):
    shape = (NLAT, 8, 128)
    main, tail = main.reshape(shape), tail.reshape(shape)
    sub, lane = iota(shape, 1), iota(shape, 2)
    low = lane < 64

    def tails(north, south):
        return jnp.where(low, pltpu.roll(tail, north, 1), pltpu.roll(pltpu.roll(tail, south, 1), 64, 2))

    first = jnp.where(sub < 2, main, jnp.where(sub < 4, pltpu.roll(main, 7, 1), tails(4, 1)))
    second = jnp.where(
        sub < 1, pltpu.roll(main, 6, 1), jnp.where(sub < 2, pltpu.roll(main, 4, 1), tails(0, 5)))
    return jnp.stack([first, second], axis=1).reshape(2 * PIECES, 128)


def load_halo(ref, c, k, south):
    row, tail_row = (k + 2 * south, 4 + k) if k < 2 else (8 + south, 10)
    tail = ref[pl.ds(c * 128 + tail_row, L, stride=16), :]
    if south:
        tail = pltpu.roll(tail, 64, 1)
    return jnp.concatenate([ref[pl.ds(c * 128 + row, L, stride=16), :], tail], axis=1)


def iota(shape, dim):
    return lax.broadcasted_iota(jnp.int32, shape, dim)


def step_kernel(
    block_in, face_in, cut_in, state_in, cx_in, cy_in, table_hbm,
    out_ref,
    block_ref, face_ref, cut_ref, state_ref, cx_ref, cy_ref,
    table, padded, main, tail, send1, got1, send2, halo,
    edges, from_west, from_east,
    tend, rows_out, rows_in, spec, spec_in, smooth_out, smooth_in,
    load_sem, table_sem, s1, r1, s2, r2, s3, r3, edge_send, edge_recv, a_send, a_recv, y_send, y_recv, b_send, b_recv,
):
    lat, lon = lax.axis_index("lat"), lax.axis_index("lon")
    half, seat = lon // HALF, lon % HALF
    partner = (lon + HALF) % NLONDEV
    east, west = (lon + 1) % NLONDEV, (lon + NLONDEV - 1) % NLONDEV

    barrier = pltpu.get_barrier_semaphore()

    @pl.loop(1, NLAT)
    def _(i):
        pl.semaphore_signal(barrier, inc=1, device_id={"lat": (lat + i) % NLAT}, device_id_type=MESH)

    @pl.loop(1, NLONDEV)
    def _(i):
        pl.semaphore_signal(barrier, inc=1, device_id={"lon": (lon + i) % NLONDEV}, device_id_type=MESH)

    loads = [
        pltpu.make_async_copy(source, target, load_sem.at[i])
        for i, (source, target) in enumerate([
            (state_in, state_ref), (cy_in, cy_ref), (face_in, face_ref),
            (block_in, block_ref), (cx_in, cx_ref), (cut_in, cut_ref)])
    ]
    for load in loads:
        load.start()
    main[...] = jnp.zeros_like(main)
    tail[...] = jnp.zeros_like(tail)
    load_table = pltpu.make_async_copy(table_hbm, table, table_sem)
    for load in loads[:4]:
        load.wait()

    cols, keep = [], []
    for t in range(2 * S):
        n = face_ref[t // S, t % S]
        safe = jnp.maximum(n, 0)
        cols.append(jnp.where(n >= 0, 8 * lax.div(safe, S) + lax.rem(safe, S) + (t // S) * S, -1))
        keep.append(jnp.where(n >= 0, 1.0, 0.0))
    keep = keep[S:]
    blocks = [block_ref[s] for s in range(S)]
    polar = [jnp.where(b < POLAR, 1, 0) + jnp.where(b >= NBLK - POLAR, 1, 0) for b in blocks]
    first = (1 - polar[0]) * polar[2]
    picks = [first, 1 + polar[2], 2 - first - polar[2]]
    asks = [
        jnp.where(picks[t % S] == 0, cols[t // S * S], jnp.where(picks[t % S] == 1, cols[t // S * S + 1], cols[t // S * S + 2]))
        for t in range(2 * S)
    ]

    lane = iota((L, LANES), 1)
    zeros = jnp.zeros((L, LANES - W), jnp.float32)

    for t in range(2 * S):
        s = t % S
        want = jnp.full((L, LANES), asks[t].astype(jnp.float32), jnp.float32)
        for f in range(F):
            row = jnp.concatenate([state_ref[f, s, NR - 1 if t < S else 0], zeros], axis=1)
            store_rows(main, tail, f, t, jnp.where(lane == W, want, row))
        if t < S:
            last_wind = jnp.concatenate([cy_ref[s, NR - 1], zeros], axis=1)
            store_rows(main, tail, F, t, jnp.where(lane == W, want, last_wind))
        else:
            store_rows(main, tail, F, t, jnp.where(lane == W, want, 0.0))

    send1[...] = pack(main[...], tail[...])

    pl.semaphore_wait(barrier, NLAT - 1 + NLONDEV - 1)

    def send_pieces(source, target, send_sem, recv_sem, start, size):
        def piece(ref, i):
            return ref.at[pl.ds(pl.multiple_of(i * 16 + start, 8), size), :]

        @pl.loop(0, NLAT - 1)
        def _(i):
            turn = i // 4
            along = 6 + (1 - 2 * (turn % 2)) * ((turn + 1) // 2)
            to = ((lat // 12 + 3 - i % 4) % 4) * 12 + (lat % 12 + along) % 12
            pltpu.make_async_remote_copy(
                piece(source, to), piece(target, lat), send_sem, recv_sem,
                device_id={"lat": to}, device_id_type=MESH).start()

    def wait_pieces(sem, ref, size):
        whole = ref.at[pl.ds(0, size * (NLAT - 1)), :]
        pltpu.make_async_copy(whole, whole, sem).wait()

    mine = pl.ds(pl.multiple_of(lat * 16, 16), 16)
    send_pieces(send1, got1, s1, r1, 0, 9)
    got1[mine, :] = send1[mine, :]

    for load in loads[4:]:
        load.wait()
    narrow = iota((L, 128), 1)

    def lane_of(f, s, r):
        return (f * S + s) * NR + r

    def put_edges(f, ends):
        left, right = ends
        for s in range(S):
            for r in range(NR):
                n = lane_of(f, s, r)
                row = state_ref[f, s, r]
                last = jnp.concatenate([row[:, 128:], zeros], axis=1)
                left = jnp.where(narrow == n, pltpu.roll(row[:, :128], n, 1), left)
                right = jnp.where(narrow == n, pltpu.roll(last, (n + 128 - (W - 1 - 128)) % 128, 1), right)
        return left, right

    nothing = jnp.zeros((L, 128), jnp.float32)
    edges[0], edges[1] = lax.fori_loop(0, F, put_edges, (nothing, nothing))
    right = nothing
    for s in range(S):
        for r in range(NR):
            n = s * NR + r
            last = jnp.concatenate([cx_ref[s, r][:, 128:], zeros], axis=1)
            right = jnp.where(narrow == n, pltpu.roll(last, (n + 128 - (W - 1 - 128)) % 128, 1), right)
    edges[2] = right

    to_west = pltpu.make_async_remote_copy(
        edges, from_east, edge_send.at[0], edge_recv.at[0], device_id={"lon": west}, device_id_type=MESH)
    to_east = pltpu.make_async_remote_copy(
        edges, from_west, edge_send.at[1], edge_recv.at[1], device_id={"lon": east}, device_id_type=MESH)
    to_west.start()
    to_east.start()


    load_table.start()
    padded[...] = jnp.zeros_like(padded)
    padded[:, :W] = state_ref[...].reshape(F * S * NR * L, W)
    rows_out[...] = jnp.zeros_like(rows_out)

    def tile(f, s, r):
        return padded[pl.ds(pl.multiple_of(((f * S + s) * NR + r) * L, L), L), :]

    to_west.wait()
    to_east.wait()

    def tend_row(f, s, r):
        return pl.ds(pl.multiple_of(((s * F + f) * NR + r) * L, L), L)

    def put_tendency(f, s, r, here, merid):
        n = lane_of(f, s, r)
        zonal = jnp.concatenate([cx_ref[s, r], zeros], axis=1)
        beyond = jnp.concatenate([nothing, pltpu.roll(from_east[0], (128 + (W - 1 - 128) - n) % 128, 1)], axis=1)
        to_the_east = jnp.where(lane == W - 1, beyond, pltpu.roll(here, LANES - 1, 1))
        across = zonal * (here + to_the_east) * 0.5
        before = pltpu.roll(from_west[1], (128 - n) % 128, 1)
        cw = pltpu.roll(from_west[2], (128 - s * NR - r) % 128, 1)
        inflow = jnp.concatenate([cw * (before + here[:, :128]) * 0.5, nothing], axis=1)
        from_the_west = jnp.where(lane == 0, inflow, pltpu.roll(across, 1, 1))
        tend[tend_row(f, s, r), :] = jnp.where(lane < W, -((across - from_the_west) + merid), 0.0)

    def wind(s, r):
        return jnp.concatenate([cy_ref[s, r], zeros], axis=1)

    for s in range(S):
        @pl.loop(0, F)
        def _(f):
            here = tile(f, s, 1)
            flux = wind(s, 0) * (tile(f, s, 0) + here) * 0.5
            for r in range(1, NR - 1):
                after = tile(f, s, r + 1)
                next_flux = wind(s, r) * (here + after) * 0.5
                put_tendency(f, s, r, here, next_flux - flux)
                flux, here = next_flux, after

    def spot(r, k, f):
        if 0 < r < NR - 1:
            n = ((r - 1) * 2 + k) * F + f
            return (n // 8) * ROWS + (n % 8) * L
        n = ((r // (NR - 1)) * 2 + k) * F + f
        return (n // 3) * ROWS + INNER + (n % 3) * L

    def spot_rows(r, k, f):
        return pl.ds(pl.multiple_of(spot(r, k, f), L), L)

    uppers = [jnp.full((L, LANES), picks[k], jnp.int32) == k + 1 for k in range(2)]

    def gather_rows(rs):
        for k in range(2):
            @pl.loop(0, F)
            def _(f):
                for r in rs:
                    low, high = tend[tend_row(f, k, r), :], tend[tend_row(f, k + 1, r), :]
                    rows_out[spot_rows(r, k, f), :] = jnp.where(uppers[k], high, low)

    starts, sizes = (0, INNER), (INNER, ROWS - INNER)

    def part(g, i):
        return pl.ds(pl.multiple_of(i * ROWS + starts[g], L), sizes[g])

    def seat_copy(g, i, source, target, send_sem, recv_sem):
        to = (seat + i) % HALF
        return pltpu.make_async_remote_copy(
            source.at[part(g, to), :], target.at[part(g, seat), :], send_sem.at[g, to], recv_sem.at[g, seat],
            device_id={"lon": half * HALF + to}, device_id_type=MESH)

    def seat_wait(g, i, source, target, send_sem, recv_sem):
        other = (seat + HALF - i) % HALF
        pltpu.make_async_remote_copy(
            source.at[part(g, other), :], target.at[part(g, other), :], send_sem.at[g, other],
            recv_sem.at[g, other], device_id={"lon": half * HALF + other}, device_id_type=MESH).wait_recv()

    there = (rows_out, rows_in, a_send, a_recv)
    back = (smooth_out, smooth_in, b_send, b_recv)

    def exchange(g, way):
        for i in (4, 5, 3, 6, 2, 7, 1):
            seat_copy(g, i, *way).start()
        way[1][part(g, seat), :] = way[0][part(g, seat), :]

    def arrive(g, way):
        for i in range(1, HALF):
            seat_wait(g, i, *way)

    def leave(g, way):
        for i in range(1, HALF):
            seat_copy(g, i, *way).wait_send()

    nn, nt = ((1,), (0,)), ((1,), (1,))

    def product(xh, xl, d, dims):
        rows = xh.shape[0]
        both = dot(jnp.concatenate([xh, xl], axis=0), table[0, d], dims)
        return both[:rows] + (both[rows:] + dot(xh, table[1, d], dims))

    def forward(g):
        total = jnp.zeros((sizes[g], 2 * KCUT), jnp.float32)
        for d in range(HALF):
            xh, xl = split2(rows_in[d * ROWS + starts[g]:d * ROWS + starts[g] + sizes[g], :])
            total += product(xh, xl, d, nn)
        spec[starts[g]:starts[g] + sizes[g], :] = total

    def swap(g):
        rows = pl.ds(starts[g], sizes[g])
        return pltpu.make_async_remote_copy(
            spec.at[rows, :], spec_in.at[rows, :], y_send.at[g], y_recv.at[g],
            device_id={"lon": partner}, device_id_type=MESH)

    chosen = [jnp.where(picks[k] == k + 1, blocks[k + 1], blocks[k]) for k in range(2)]

    def limits(g):
        parts = []
        for j in range(sizes[g] // L):
            if g == 0:
                n = seat * 8 + j
                r = 1 + n // (2 * F)
            else:
                n = seat * 3 + j
                r = jnp.minimum(n // (2 * F), 1) * (NR - 1)
            block = jnp.where((n // F) % 2 == 0, chosen[0], chosen[1])
            parts.append(jnp.full((L, 2 * KCUT), cut_ref[block * NR + r], jnp.int32))
        return jnp.concatenate(parts, axis=0)

    def inverse(g):
        shape = (sizes[g], 2 * KCUT)
        wave = iota(shape, 1) % KCUT
        sign = jnp.where(wave % 2 == 0, 1.0, -1.0)
        scale = jnp.where(wave == 0, 1.0 / NLON, 2.0 / NLON)
        rows = slice(starts[g], starts[g] + sizes[g])
        weights = jnp.where(wave < limits(g), scale, 0.0)
        xh, xl = split2((spec[rows, :] + sign * spec_in[rows, :]) * weights)
        for d in range(HALF):
            smooth_out[d * ROWS + starts[g]:d * ROWS + starts[g] + sizes[g], :] = product(xh, xl, d, nt)

    gather_rows(range(1, NR - 1))
    exchange(0, there)

    wait_pieces(r1, got1, 9)
    pieces = jnp.concatenate(unpack(got1[...]), axis=1)
    asked = jnp.broadcast_to(pieces[:, W:W + 1], (PIECES, PIECES))
    onehot = jnp.where(asked == iota((PIECES, PIECES), 1).astype(jnp.float32), 1.0, 0.0).astype(jnp.bfloat16)
    a, b, c = split3(pieces)
    found = (dot(onehot, a, nn) + dot(onehot, b, nn)) + dot(onehot, c, nn)
    send2[...] = pack_asked(found[:, :128], found[:, 128:])
    send_pieces(send2, halo, s2, r2, 0, 6)
    halo[mine, :] = send2[mine, :]

    load_table.wait()
    arrive(0, there)
    forward(0)
    swap(0).start()
    send_pieces(send2, halo, s3, r3, 8, 3)

    at_pick = [[jnp.full((L, LANES), picks[k], jnp.int32) == s for k in range(S)] for s in range(S)]

    def outer_rows(known):
        for s in range(S):
            kept = jnp.full((L, LANES), keep[s], jnp.float32)

            def halo_row(c, south):
                row = load_halo(halo, c, 1, south)
                for k in known:
                    row = jnp.where(at_pick[s][k], load_halo(halo, c, k, south), row)
                return row

            @pl.loop(0, F)
            def _(f):
                above, below, north_wind = halo_row(f, 0), halo_row(f, 1), halo_row(F, 0)
                here, after = tile(f, s, 0), tile(f, s, 1)
                put_tendency(
                    f, s, 0, here, wind(s, 0) * (here + after) * 0.5 - north_wind * (above + here) * 0.5)
                before, here = tile(f, s, NR - 2), tile(f, s, NR - 1)
                put_tendency(
                    f, s, NR - 1, here,
                    wind(s, NR - 1) * (here + below) * 0.5 * kept - wind(s, NR - 2) * (before + here) * 0.5)

    wait_pieces(r2, halo, 6)
    outer_rows((0,))
    gather_rows((0, NR - 1))
    exchange(1, there)

    swap(0).wait()
    inverse(0)
    exchange(0, back)

    arrive(1, there)
    forward(1)
    swap(1).start()
    wait_pieces(r3, halo, 3)
    outer_rows((0, 2))
    swap(1).wait()
    inverse(1)
    exchange(1, back)

    uses = [
        [jnp.full((L, LANES), jnp.where(picks[k] == s, polar[s], 0), jnp.int32) > 0 for k in range(2)]
        for s in range(S)
    ]

    def finish(rs):
        for s in range(S):
            @pl.loop(0, F)
            def _(f):
                for r in rs:
                    value = tend[tend_row(f, s, r), :]
                    for k in range(2):
                        value = jnp.where(uses[s][k], smooth_in[spot_rows(r, k, f), :], value)
                    out_ref[f, s, r] = value[:, :W]

    arrive(0, back)
    finish(range(1, NR - 1))
    arrive(1, back)
    finish((0, NR - 1))

    wait_pieces(s1, send1, 9)
    wait_pieces(s2, send2, 6)
    wait_pieces(s3, send2, 3)
    for g in range(2):
        leave(g, there)
        leave(g, back)


def shards(table, state, courant_x, courant_y, block_of_slot, face_source, cutoff):
    vmem = pl.BlockSpec(memory_space=pltpu.VMEM)
    i32 = jnp.int32
    f32 = jnp.float32
    rows = F * S * NR * L
    dma = pltpu.SemaphoreType.DMA
    filtered = pl.pallas_call(
        step_kernel,
        out_shape=jax.ShapeDtypeStruct((F, S, NR, L, W), f32),
        in_specs=[pl.BlockSpec(memory_space=pltpu.HBM)] * 7,
        out_specs=vmem,
        scratch_shapes=[
            pltpu.SMEM((S,), i32),
            pltpu.SMEM((2, S), i32),
            pltpu.SMEM((NBLK * NR,), i32),
            pltpu.VMEM((F, S, NR, L, W), f32),
            pltpu.VMEM((S, NR, L, W), f32),
            pltpu.VMEM((S, NR, L, W), f32),
            pltpu.VMEM((2, HALF, LANES, 2 * KCUT), jnp.bfloat16),
            pltpu.VMEM((rows, LANES), f32),
            pltpu.VMEM((PIECES, 128), f32),
            pltpu.VMEM((PIECES, 128), f32),
            pltpu.VMEM((2 * PIECES, 128), f32),
            pltpu.VMEM((2 * PIECES, 128), f32),
            pltpu.VMEM((2 * PIECES, 128), f32),
            pltpu.VMEM((2 * PIECES, 128), f32),
            pltpu.VMEM((3, L, 128), f32),
            pltpu.VMEM((3, L, 128), f32),
            pltpu.VMEM((3, L, 128), f32),
            pltpu.VMEM((rows, LANES), f32),
            pltpu.VMEM((HALF * ROWS, LANES), f32),
            pltpu.VMEM((HALF * ROWS, LANES), f32),
            pltpu.VMEM((ROWS, 2 * KCUT), f32),
            pltpu.VMEM((ROWS, 2 * KCUT), f32),
            pltpu.VMEM((HALF * ROWS, LANES), f32),
            pltpu.VMEM((HALF * ROWS, LANES), f32),
            dma((6,)), dma, dma, dma, dma, dma, dma, dma,
            dma((2,)), dma((2,)),
            dma((2, HALF)), dma((2, HALF)),
            dma((2,)), dma((2,)),
            dma((2, HALF)), dma((2, HALF)),
        ],
        compiler_params=pltpu.CompilerParams(
            collective_id=0, has_side_effects=True, vmem_limit_bytes=48 << 20),
    )(block_of_slot, face_source.T, cutoff, state, courant_x, courant_y, table)
    return state + filtered


def solution(mesh):
    placed = (
        P(),
        P(None, "lat", None, None, "lon"),
        P("lat", None, None, "lon"),
        P("lat", None, None, "lon"),
        P("lat"),
        P("lat", None),
        P(),
    )
    body = jax.shard_map(
        shards,
        mesh=mesh,
        in_specs=placed,
        out_specs=P(None, "lat", None, None, "lon"),
        check_vma=False,
    )
    table = basis_table()
    return lambda *arrays: body(jnp.asarray(table), *arrays)
```
